256 devices in a mesh: arc: 8 (over z), tile: 32 (over x, y, core).
Axes of the slice: x: 4, y: 4, z: 8, core: 2. Of those that a mesh axis runs over, the one named last changes fastest.
Arguments:
- design: bfloat16 [2048, 128, 512], P(('arc', 'tile')), may hold values from -0.059814453 to 0.059814453
- observed: float32 [2048, 128], P(('arc', 'tile')), may hold values from -6 to 6
- obs_type: int32 [2048, 128], P(('arc', 'tile')), may hold values from 0 to 7
- owner_of: int32 [2048, 4], P(('arc', 'tile')), may hold values from 0 to 31, all different within a row; in each aligned block of 8 rows (0 to 7, 8 to 15, ...) at most 2 rows name the same one
- sub_of: int32 [2048, 4], P(('arc', 'tile')), may hold values from 0 to 2
- sigma_table: float32 [8], replicated, may hold values from 0.3 to 3
- solution: float32 [12288], P('tile'), may hold values from -6 to 6
- prior: float32 [12288, 12288], P('arc', 'tile'), may hold values from -0.6 to 0.6
Outputs:
- normal_matrix: float32 [12288, 12288], P('arc', 'tile')
- gradient: float32 [12288], P('tile')
The draws below stay inside these ranges and needn't reach their ends.
Inputs may be any that keep to these rules, and one draw needn't show every extreme that they name: `owner_of`: each block names 4 different owners. Among the 8 blocks of one device no owner is named more than 2 times, a bound that some block reaches in every draw.
All inputs are finite; a program needn't handle non-finite values.
Results may differ from the reference program's by a relative error of at most 0.006.
Values may be sent and summed in bfloat16 or wider, within the bound.
No kernel may reach another device: no remote copies, remote signals or barrier semaphores. Data moves between devices by JAX's collectives and lax.ppermute only.
A program may use at most 128 MiB of HBM per device.

```python
import math
import jax
import jax.numpy as jnp
import numpy as np
from jax import lax

P_SIZE = 12288
TW = 128
ROWS = 128
NTYPES = 8
NB = 8
TPO = 3
CAP = 2
BLOCKS = 2048
N_ARC = 8
N_TILE = 32


def touch_ends(array, stream_key, smallest, top_value):
    spot = [jax.random.randint(jax.random.fold_in(stream_key, axis), (), 0, length) for axis, length in enumerate(array.shape)]
    main_axis = array.shape.index(max(array.shape))
    next_to = spot[:main_axis] + [(spot[main_axis] + 1) % array.shape[main_axis]] + spot[main_axis + 1:]
    return array.at[tuple(spot)].set(smallest).at[tuple(next_to)].set(top_value)


def shard_levels(rng, shape, cuts, smallest, high):
    factor_of, own = 1.0, jax.random.fold_in(rng, 6)
    for position, parts in cuts:
        heights = jnp.exp(jax.random.uniform(jax.random.fold_in(own, position), (parts,), jnp.float32, smallest / len(cuts), high / len(cuts)))
        factor_of = factor_of * jnp.repeat(heights, shape[position] // parts).reshape([-1 if axis == position else 1 for axis in range(len(shape))])
    return factor_of


def shared_out(key, own, number, rows, amount, top, most, slope):
    ranking = jax.random.permutation(key, amount)
    packed, usual = shares(amount, rows * top, most, slope, True), shares(amount, rows * top, most, slope, False)
    places = jnp.arange(amount)

    def named(lengths, offset_by):
        used = int((lengths > 0).sum())
        fixed = max(1, used // 4)
        shifted = fixed + (places - fixed + offset_by * (used - fixed)) % max(1, amount - fixed)
        return jnp.zeros((amount,), jnp.int32).at[ranking[jnp.where(places < fixed, places, shifted)]].set(jnp.asarray(lengths, jnp.int32))

    lengths = jnp.where(number % 4 == 0, named(packed, number // 4), named(usual, number - number // 4 - 1))
    mixed = jax.random.permutation(jax.random.fold_in(own, 3), amount)
    donor, taker = mixed[0:amount // 2 * 2:2], mixed[1:amount // 2 * 2:2]
    margin = jnp.minimum(lengths[donor] - 1, most - lengths[taker]) // 2
    margin = jnp.where((donor == ranking[0]) | (taker == ranking[0]) | (lengths[taker] == 0), 0, jnp.maximum(margin, 0))
    shifted = jax.random.randint(jax.random.fold_in(own, 4), (amount // 2,), 0, 1 << 20) % (margin + 1)
    lengths = lengths.at[donor].add(-shifted).at[taker].add(shifted)
    members = jnp.searchsorted(jnp.cumsum(lengths), jnp.arange(rows * top), side="right").astype(jnp.int32)
    table = members.reshape(top, rows).T
    table = table[jax.random.permutation(jax.random.fold_in(own, 1), rows)]
    offset_by = jax.random.randint(jax.random.fold_in(own, 2), (rows, 1), 0, top)
    return jnp.take_along_axis(table, (jnp.arange(top)[None, :] + offset_by) % top, axis=1)


def shares(count, total, limit, skew, full):
    loads = [(1 << 20) // math.isqrt(standing ** skew) + 1 for standing in range(1, count + 1)]
    largest = limit if full else min(limit, max(-(-total // count), total * loads[0] // sum(loads)))
    least = 1 if total - largest >= count - 1 else 0
    given, spare = [largest] + [least] * (count - 1), total - largest - least * (count - 1)
    while spare > 0:
        candidates = [i for i in range(1, count) if given[i] < largest] or [i for i in range(1, count) if given[i] < limit]
        pool, remaining = sum([loads[i] for i in candidates]), spare
        for i in candidates:
            more = min(limit - given[i], max(1, remaining * loads[i] // pool), spare)
            given[i] = given[i] + more
            spare = spare - more
    return np.array(given)


def centred(rng, dims, deviation, bound, pieces=(), kind=jnp.bfloat16):
    drawn = deviation * jax.random.normal(rng, dims, jnp.float32)
    if pieces:
        drawn = drawn * shard_levels(rng, dims, pieces, -0.22, 0.18)
    return jnp.clip(drawn, -bound, bound).astype(kind)


def setup_inputs(seed: int = 0) -> dict:
    key_list = jax.random.split(jax.random.key(seed), 9)
    design = centred(key_list[0], (BLOCKS, ROWS, 4 * TW), 0.01, 0.059814453, ((0, 256),))
    observed = centred(key_list[1], (BLOCKS, ROWS), 1.0, 6.0, ((0, 256),), jnp.float32)
    obs_type = touch_ends(jax.random.randint(key_list[2], (BLOCKS, ROWS), 0, NTYPES), jax.random.fold_in(key_list[2], 1), 0, NTYPES - 1).astype(jnp.int32)
    owner_of_keys = jax.random.split(jax.random.fold_in(key_list[3], 1), BLOCKS // NB)
    owner_of_turns = jax.random.permutation(jax.random.fold_in(key_list[3], 3), BLOCKS // NB)
    owner_of = jax.vmap(lambda own, number: shared_out(jax.random.fold_in(key_list[3], 2), own, number, NB, N_TILE, 4, CAP, 2))(owner_of_keys, owner_of_turns).reshape((BLOCKS, 4))
    sub_of = touch_ends(jax.random.randint(key_list[4], (BLOCKS, 4), 0, TPO), jax.random.fold_in(key_list[4], 1), 0, TPO - 1).astype(jnp.int32)
    sigma_table = jnp.clip(jnp.exp(jax.random.uniform(key_list[5], (NTYPES,), jnp.float32, math.log(0.3), math.log(3.0))), 0.3, 3.0)
    solution = centred(key_list[6], (P_SIZE,), 1.0, 6.0, ((0, 32),), jnp.float32)
    prior = centred(key_list[7], (P_SIZE, P_SIZE), 0.1, 0.6, ((0, 8), (1, 32)), jnp.float32)
    return dict(design=design, observed=observed, obs_type=obs_type, owner_of=owner_of, sub_of=sub_of, sigma_table=sigma_table, solution=solution, prior=prior)


huber_limit = 1.345

def block_terms(design_block, observed_block, type_block, block_tiles, solution, sigma_table):
    tile_width = design_block.shape[1] // 4
    design_tiles = design_block.reshape(design_block.shape[0], 4, tile_width).astype(jnp.float32)
    touched = solution.reshape(-1, tile_width)[block_tiles]
    predicted = jnp.einsum('qlc,lc->q', design_tiles, touched, precision=lax.Precision.HIGHEST)
    residual = observed_block - predicted
    type_ids = jnp.arange(sigma_table.shape[0], dtype=jnp.int32)
    spread = lax.optimization_barrier(jnp.sum(jnp.where(type_block[:, None] == type_ids[None, :], sigma_table[None, :], 0.0), axis=1))
    scaled = jnp.abs(residual) / spread
    root_weight = jnp.sqrt(huber_limit / jnp.maximum(scaled, huber_limit)) / spread
    weighted = lax.optimization_barrier((root_weight[:, None, None] * design_tiles).astype(jnp.bfloat16)).astype(jnp.float32)
    target = lax.optimization_barrier((root_weight * residual).astype(jnp.bfloat16)).astype(jnp.float32)
    gram_tiles = jnp.einsum('qlc,qmr->lmcr', weighted, weighted, precision=lax.Precision.HIGHEST)
    pull_terms = jnp.einsum('qlc,q->lc', weighted, target, precision=lax.Precision.HIGHEST)
    return (gram_tiles, pull_terms)

def reference(design, observed, obs_type, owner_of, sub_of, sigma_table, solution, prior):
    tile_count = P_SIZE // TW
    per_owner = tile_count // N_TILE
    tile_ids = owner_of * per_owner + sub_of
    group_blocks = BLOCKS // N_ARC
    grouped = (design.reshape(N_ARC, group_blocks, ROWS, 4 * TW), observed.reshape(N_ARC, group_blocks, ROWS), obs_type.reshape(N_ARC, group_blocks, ROWS), tile_ids.reshape(N_ARC, group_blocks, 4))

    def block_step(state_pair, block_data):
        partial_value, grad_total = state_pair
        design_block, observed_block, type_block, block_tiles = block_data
        gram_tiles, pull_terms = block_terms(design_block, observed_block, type_block, block_tiles, solution, sigma_table)
        partial_value = partial_value.at[block_tiles[:, None], :, block_tiles[None, :], :].add(gram_tiles)
        grad_total = grad_total.at[block_tiles].add(pull_terms)
        return ((partial_value, grad_total), None)

    def group_step(state_pair, group_data):
        normal_total, grad_total = state_pair
        empty = jnp.zeros((tile_count, TW, tile_count, TW), jnp.float32)
        (partial_value, grad_total), unused = lax.scan(block_step, (empty, grad_total), group_data)
        rounded = lax.optimization_barrier(partial_value.astype(jnp.bfloat16)).astype(jnp.float32)
        return ((normal_total + rounded, grad_total), None)
    initial = (jnp.zeros((tile_count, TW, tile_count, TW), jnp.float32), jnp.zeros((tile_count, TW), jnp.float32))
    (normal_total, grad_total), unused = lax.scan(group_step, initial, grouped)
    return (prior + normal_total.reshape(P_SIZE, P_SIZE), grad_total.reshape(P_SIZE))
```

```python
import functools

import jax
import jax.numpy as jnp
from jax import lax
from jax.experimental import pallas as pl
from jax.experimental.pallas import tpu as pltpu
from jax.sharding import PartitionSpec as P

HUBER = 1.345
TW = 128
SLOTS = 2
HEAD = 16
CHUNKS = 2
F32 = jnp.float32
BF16 = jnp.bfloat16
NT = (((1,), (1,)), ((), ()))


def pack_kernel(
    owner_ref, ids_ref, sigma_ref, design_ref, observed_ref, type_ref, sol_ref, *refs
):
    outs, (dt_ref, head_ref, table_ref) = refs[:-3], refs[-3:]
    blocks = observed_ref.shape[0]
    step = pl.program_id(0)
    group = outs[0].shape[0]
    part = TW // len(outs)

    @pl.when(step == 0)
    def _():
        n_slot = table_ref.shape[0]

        @pl.loop(0, n_slot)
        def _(i):
            table_ref[i] = -1

        @pl.loop(0, blocks * 4)
        def _(i):
            first = owner_ref[i] * SLOTS
            table_ref[jnp.where(table_ref[first] < 0, first, first + 1)] = i

        head_ref[...] = jnp.zeros_like(head_ref)
        spread = jnp.zeros(observed_ref.shape, F32)
        for k in range(sigma_ref.shape[0]):
            spread = jnp.where(type_ref[...] == k, sigma_ref[k], spread)
        for b in range(blocks):
            predicted = jnp.zeros((1, TW), F32)
            for l in range(4):
                tile = design_ref[b, :, l * TW : (l + 1) * TW].astype(F32).T
                s = sol_ref[pl.ds(ids_ref[b * 4 + l], 1), :]
                s = jnp.broadcast_to(s, (8, TW))
                predicted += jnp.dot(
                    s, tile, precision=lax.Precision.HIGHEST, preferred_element_type=F32
                )[0:1]
                dt_ref[b * 4 + l] = tile.astype(BF16)
            residual = observed_ref[b : b + 1] - predicted
            spr = spread[b : b + 1]
            scaled = jnp.abs(residual) / spr
            root = jnp.sqrt(HUBER / jnp.maximum(scaled, HUBER)) / spr
            head_ref[b, 0:1, :] = (root * residual).astype(BF16)
            for l in range(4):
                dt_ref[b * 4 + l] = (root * dt_ref[b * 4 + l].astype(F32)).astype(BF16)

    @pl.loop(0, group)
    def _(g):
        item = table_ref[step * group + g]

        @pl.when(item >= 0)
        def _():
            b = item // 4
            m = item - b * 4
            outs[0][g, 0:TW, :] = dt_ref[item]
            outs[0][g, TW : TW + HEAD, :] = head_ref[b]
            for r in range(3):
                other = b * 4 + lax.rem(m + r + 1, 4)
                for j, out in enumerate(outs):
                    base = (TW + HEAD if j == 0 else 0) + r * part
                    out[g, base : base + part, :] = dt_ref[
                        other, j * part : (j + 1) * part, :
                    ]


def pack(owner, ids, sigma, design, observed, obs_type, sol, n_owner):
    n_slot = n_owner * SLOTS
    part = TW // CHUNKS
    group = 8
    rows = [TW + HEAD + 3 * part] + [3 * part] * (CHUNKS - 1)
    blocks = observed.shape[0]
    whole = lambda *shape: pl.BlockSpec(shape, lambda i, *_: (0,) * len(shape))
    return pl.pallas_call(
        pack_kernel,
        grid_spec=pltpu.PrefetchScalarGridSpec(
            num_scalar_prefetch=3,
            grid=(n_slot // group,),
            in_specs=[
                whole(*design.shape),
                whole(*observed.shape),
                whole(*obs_type.shape),
                whole(*sol.shape),
            ],
            out_specs=[pl.BlockSpec((group, r, TW), lambda i, *_: (i, 0, 0)) for r in rows],
            scratch_shapes=[
                pltpu.VMEM((blocks * 4, TW, TW), BF16),
                pltpu.VMEM((blocks, HEAD, TW), BF16),
                pltpu.SMEM((n_slot,), jnp.int32),
            ],
        ),
        out_shape=[jax.ShapeDtypeStruct((n_slot, r, TW), BF16) for r in rows],
        name="pack",
    )(owner, ids, sigma, design, observed, obs_type, sol)


def gather_kernel(chunk, table_ref, *refs):
    first = chunk == 0
    if first:
        main_ref, panel_ref, grad_ref, acc_ref = refs
        side_ref = main_ref
    else:
        main_ref, side_ref, panel_ref, acc_ref = refs
    group = main_ref.shape[0]
    part = panel_ref.shape[1]
    base = TW + HEAD if first else 0
    step = pl.program_id(0)

    @pl.when(step == 0)
    def _():
        acc_ref[...] = jnp.zeros_like(acc_ref)
        if first:
            grad_ref[...] = jnp.zeros_like(grad_ref)

    @pl.loop(0, group)
    def _(g):
        item = (step * group + g) * 6

        @pl.when(table_ref[item] > 0)
        def _():
            own = main_ref[g, 0:TW, :]
            if first:
                side = side_ref[g, TW : base + 3 * part, :]
            else:
                side = side_ref[g]
            prod = lax.dot_general(side, own, NT, preferred_element_type=F32)
            diag = lax.dot_general(
                main_ref[g, chunk * part : (chunk + 1) * part, :],
                own,
                NT,
                preferred_element_type=F32,
            )
            acc_ref[table_ref[item + 2]] += diag
            skip = HEAD if first else 0
            for r in range(3):
                acc_ref[table_ref[item + 3 + r]] += prod[
                    skip + r * part : skip + (r + 1) * part
                ]
            if first:
                sub = table_ref[item + 1]
                grad_ref[pl.ds(sub, 1), :] += prod[0:1]

    @pl.when(step == pl.num_programs(0) - 1)
    def _():
        @pl.loop(0, acc_ref.shape[0])
        def _(i):
            panel_ref[i] = acc_ref[i].astype(BF16)


def gather(chunk, table, got, n_tile_slots):
    part = TW // CHUNKS
    group = 8
    n_slot = got[0].shape[0]
    main_rows = got[0].shape[1] if chunk == 0 else TW
    in_specs = [pl.BlockSpec((group, main_rows, TW), lambda i, *_: (i, 0, 0))]
    args = [got[0]]
    out_specs = [pl.BlockSpec((n_tile_slots, part, TW), lambda i, *_: (0, 0, 0))]
    out_shape = [jax.ShapeDtypeStruct((n_tile_slots, part, TW), BF16)]
    if chunk == 0:
        out_specs.append(pl.BlockSpec((8, TW), lambda i, *_: (0, 0)))
        out_shape.append(jax.ShapeDtypeStruct((8, TW), F32))
    else:
        in_specs.append(pl.BlockSpec((group, 3 * part, TW), lambda i, *_: (i, 0, 0)))
        args.append(got[chunk])
    return pl.pallas_call(
        functools.partial(gather_kernel, chunk),
        grid_spec=pltpu.PrefetchScalarGridSpec(
            num_scalar_prefetch=1,
            grid=(n_slot // group,),
            in_specs=in_specs,
            out_specs=out_specs,
            scratch_shapes=[pltpu.VMEM((n_tile_slots, part, TW), F32)],
        ),
        out_shape=out_shape,
        name=f"gather{chunk}",
    )(table, *args)


def final_kernel(prior_ref, *refs):
    reds, out_ref = refs[:-1], refs[-1]
    part = TW // len(reds)
    per = reds[0].shape[0]
    for j, red in enumerate(reds):
        rows = slice(j * part, (j + 1) * part)
        for s in range(per):
            cols = slice(s * TW, (s + 1) * TW)
            out_ref[rows, cols] = prior_ref[rows, cols] + red[s, 0].astype(F32)


def final(prior, reds):
    n_row = prior.shape[0] // TW
    per, _, part, _ = reds[0].shape
    spec = pl.BlockSpec((TW, prior.shape[1]), lambda i: (i, 0))
    return pl.pallas_call(
        final_kernel,
        grid=(n_row,),
        in_specs=[spec]
        + [pl.BlockSpec((per, 1, part, TW), lambda i: (0, i, 0, 0))] * len(reds),
        out_specs=spec,
        out_shape=jax.ShapeDtypeStruct(prior.shape, F32),
        name="final",
    )(prior, *reds)


def on_device(design, observed, obs_type, owner_of, sub_of, sigma_table, solution, prior):
    n_owner = lax.axis_size("tile")
    n_arc = lax.axis_size("arc")
    blocks = design.shape[0]
    per_owner = solution.shape[0] // TW
    tile_count = per_owner * n_owner
    row_tiles = tile_count // n_arc
    own_index = lax.axis_index("tile")

    tile_ids = (owner_of * per_owner + sub_of).reshape(blocks * 4)
    small = jnp.concatenate([solution, tile_ids.astype(F32)])
    small = jnp.pad(small, (0, 8 * TW - small.shape[0])).reshape(8, TW)
    everyone = lax.all_gather(small, "tile", axis=0, tiled=True).reshape(n_owner, 8, TW)
    sol = everyone[:, :per_owner].reshape(tile_count, TW)
    all_ids = everyone[:, per_owner, : blocks * 4].astype(jnp.int32)

    payload = pack(
        owner_of.reshape(-1), tile_ids, sigma_table, design, observed, obs_type, sol, n_owner
    )
    got = []
    for p in payload:
        p = p.reshape(n_owner, SLOTS, *p.shape[1:])
        g = lax.all_to_all(p, "tile", split_axis=0, concat_axis=0, tiled=True)
        got.append(g.reshape(n_owner * SLOTS, *p.shape[2:]))

    hit = (all_ids // per_owner == own_index).astype(jnp.int32)
    items = blocks * 4
    lower = (jnp.arange(items)[:, None] < jnp.arange(items)[None, :]).astype(jnp.int32)
    rank = jnp.sum(hit[:, :, None] * lower[None], axis=1)
    pick = hit[:, None, :] * (rank[:, None, :] == jnp.arange(SLOTS)[None, :, None]).astype(
        jnp.int32
    )
    sub = all_ids % per_owner
    grid = all_ids.reshape(n_owner, blocks, 4)
    columns = [jnp.ones_like(sub), sub]
    for r in range(4):
        ids = jnp.roll(grid, -r, axis=2).reshape(n_owner, items)
        columns.append(
            (ids // row_tiles) * (per_owner * row_tiles) + sub * row_tiles + ids % row_tiles
        )
    table = jnp.stack([jnp.sum(pick * c[:, None, :], axis=2) for c in columns], axis=2)
    table = table.reshape(-1)

    reds = []
    for j in range(CHUNKS):
        out = gather(j, table, got, tile_count * per_owner)
        if j == 0:
            grad = out[1][:per_owner].reshape(-1)
        panel = out[0].reshape(n_arc, per_owner, row_tiles, TW // CHUNKS, TW)
        red = lax.psum_scatter(panel, "arc", scatter_dimension=0, tiled=True)
        reds.append(red.reshape(panel.shape[1:]))
    gradient = lax.psum(grad, "arc")
    return final(prior, reds), gradient


def solution(mesh):
    both = ("arc", "tile")
    in_specs = (
        P(both, None, None),
        P(both, None),
        P(both, None),
        P(both, None),
        P(both, None),
        P(),
        P("tile"),
        P("arc", "tile"),
    )
    return jax.shard_map(
        on_device,
        mesh=mesh,
        in_specs=in_specs,
        out_specs=(P("arc", "tile"), P("tile")),
        check_vma=False,
    )
```

```python
import functools

import jax
import jax.numpy as jnp
from jax import lax
from jax.experimental import pallas as pl
from jax.experimental.pallas import tpu as pltpu
from jax.sharding import PartitionSpec as P

HUBER = 1.345
TW = 128
SLOTS = 2
HEAD = 16
PARTS = (48, 80)
UNROLL = 4
F32 = jnp.float32
BF16 = jnp.bfloat16
NT = (((1,), (1,)), ((), ()))


def weigh_kernel(
    ids_ref, sigma_ref, design_ref, observed_ref, type_ref, sol_ref, wt_ref, head_ref
):
    blocks = observed_ref.shape[0]
    head_ref[...] = jnp.zeros_like(head_ref)
    spread = jnp.zeros(observed_ref.shape, F32)
    for k in range(sigma_ref.shape[0]):
        spread = jnp.where(type_ref[...] == k, sigma_ref[k], spread)
    row = lax.broadcasted_iota(jnp.int32, (8, TW), 0)
    for b in range(blocks):
        predicted = jnp.zeros((8, TW), F32)
        for l in range(4):
            s = jnp.broadcast_to(sol_ref[pl.ds(ids_ref[b * 4 + l], 1), :], (8, TW))
            hi = s.astype(BF16).astype(F32)
            mid = (s - hi).astype(BF16).astype(F32)
            low = s - hi - mid
            terms = jnp.where(row == 0, hi, jnp.where(row == 1, mid, low))
            terms = jnp.where(row < 3, terms, 0.0).astype(BF16)
            predicted += lax.dot_general(
                terms,
                design_ref[b, :, l * TW : (l + 1) * TW],
                NT,
                preferred_element_type=F32,
            )
        predicted = jnp.sum(predicted, axis=0, keepdims=True)
        residual = observed_ref[b : b + 1] - predicted
        spr = spread[b : b + 1]
        scaled = jnp.abs(residual) / spr
        root = jnp.sqrt(HUBER / jnp.maximum(scaled, HUBER)) / spr
        head_ref[b, 0:1, :] = (root * residual).astype(BF16)
        for l in range(4):
            tile = design_ref[b, :, l * TW : (l + 1) * TW].T
            wt_ref[b * 4 + l] = (root * tile.astype(F32)).astype(BF16)


def weigh(ids, sigma, design, observed, obs_type, sol):
    blocks = observed.shape[0]
    vmem = pl.BlockSpec(memory_space=pltpu.VMEM)
    smem = pl.BlockSpec(memory_space=pltpu.SMEM)
    return pl.pallas_call(
        weigh_kernel,
        in_specs=[smem, smem, vmem, vmem, vmem, vmem],
        out_specs=[vmem, vmem],
        out_shape=[
            jax.ShapeDtypeStruct((blocks * 4, TW, TW), BF16),
            jax.ShapeDtypeStruct((blocks, HEAD, TW), BF16),
        ],
        name="weigh",
    )(ids, sigma, design, observed, obs_type, sol)


def pack_kernel(chunk, owner_ref, wt_ref, head_ref, out_ref, table_ref):
    step = pl.program_id(0)
    group = out_ref.shape[0]
    begin, part = sum(PARTS[:chunk]), PARTS[chunk]

    @pl.when(step == 0)
    def _():
        @pl.loop(0, table_ref.shape[0])
        def _(i):
            table_ref[i] = -1

        @pl.loop(0, wt_ref.shape[0])
        def _(i):
            first = owner_ref[i] * SLOTS
            table_ref[jnp.where(table_ref[first] < 0, first, first + 1)] = i

    @pl.loop(0, group)
    def _(g):
        item = table_ref[step * group + g]

        @pl.when(item >= 0)
        def _():
            b = item // 4
            m = item - b * 4
            base = 0
            if chunk == 0:
                out_ref[g, 0:TW, :] = wt_ref[item]
                base = TW
            if chunk == len(PARTS) - 1:
                out_ref[g, base : base + HEAD, :] = head_ref[b]
                base += HEAD
            for r in range(3):
                other = b * 4 + lax.rem(m + r + 1, 4)
                out_ref[g, base : base + part, :] = wt_ref[other, begin : begin + part, :]
                base += part


def payload_rows(chunk):
    rows = 3 * PARTS[chunk]
    return rows + TW * (chunk == 0) + HEAD * (chunk == len(PARTS) - 1)


def pack(chunk, owner, wt, head, n_owner):
    n_slot = n_owner * SLOTS
    group = 8
    rows = payload_rows(chunk)
    whole = lambda x: pl.BlockSpec(x.shape, lambda i, *_: (0, 0, 0))
    return pl.pallas_call(
        functools.partial(pack_kernel, chunk),
        grid_spec=pltpu.PrefetchScalarGridSpec(
            num_scalar_prefetch=1,
            grid=(n_slot // group,),
            in_specs=[whole(wt), whole(head)],
            out_specs=pl.BlockSpec((group, rows, TW), lambda i, *_: (i, 0, 0)),
            scratch_shapes=[pltpu.SMEM((n_slot,), jnp.int32)],
        ),
        out_shape=jax.ShapeDtypeStruct((n_slot, rows, TW), BF16),
        name=f"pack{chunk}",
    )(owner, wt, head)


def gather_kernel(chunk, table_ref, *refs):
    last = chunk == len(PARTS) - 1
    main_ref = refs[0]
    side_ref = refs[0] if chunk == 0 else refs[1]
    panel_ref = refs[1 if chunk == 0 else 2]
    grad_ref = refs[-2] if last else None
    acc_ref = refs[-1]
    group = main_ref.shape[0]
    begin, part = sum(PARTS[:chunk]), PARTS[chunk]
    skip = HEAD if last else 0
    top = TW if chunk == 0 else 0
    step = pl.program_id(0)

    @pl.when(step == 0)
    def _():
        if last:
            grad_ref[...] = jnp.zeros_like(grad_ref)

        @pl.loop(0, acc_ref.shape[0])
        def _(i):
            acc_ref[i] = jnp.zeros(acc_ref.shape[1:], F32)

    for g0 in range(0, group, UNROLL):
        prods = []
        for g in range(g0, g0 + UNROLL):
            own = main_ref[g, 0:TW, :]
            side = side_ref[g, top : top + skip + 3 * part, :]
            diag = main_ref[g, begin : begin + part, :]
            prods.append(
                [
                    lax.dot_general(x, own, NT, preferred_element_type=F32)
                    for x in (side, diag)
                ]
            )
        for u, (side, diag) in enumerate(prods):
            item = (step * group + g0 + u) * 5
            acc_ref[table_ref[item + 1]] += diag
            for r in range(3):
                acc_ref[table_ref[item + 2 + r]] += side[
                    skip + r * part : skip + (r + 1) * part
                ]
            if last:
                grad_ref[pl.ds(table_ref[item], 1), :] += side[0:1]

    @pl.when(step == pl.num_programs(0) - 1)
    def _():
        @pl.loop(0, panel_ref.shape[0])
        def _(i):
            panel_ref[i] = acc_ref[i].astype(BF16)


def gather(chunk, table, got, n_tile_slots):
    part = PARTS[chunk]
    group = 8
    n_slot = got[0].shape[0]
    main_rows = got[0].shape[1] if chunk == 0 else TW
    in_specs = [pl.BlockSpec((group, main_rows, TW), lambda i, *_: (i, 0, 0))]
    args = [got[0]]
    out_specs = [pl.BlockSpec((n_tile_slots, part, TW), lambda i, *_: (0, 0, 0))]
    out_shape = [jax.ShapeDtypeStruct((n_tile_slots, part, TW), BF16)]
    if chunk > 0:
        in_specs.append(
            pl.BlockSpec((group, payload_rows(chunk), TW), lambda i, *_: (i, 0, 0))
        )
        args.append(got[chunk])
    if chunk == len(PARTS) - 1:
        out_specs.append(pl.BlockSpec((8, TW), lambda i, *_: (0, 0)))
        out_shape.append(jax.ShapeDtypeStruct((8, TW), F32))
    return pl.pallas_call(
        functools.partial(gather_kernel, chunk),
        grid_spec=pltpu.PrefetchScalarGridSpec(
            num_scalar_prefetch=1,
            grid=(n_slot // group,),
            in_specs=in_specs,
            out_specs=out_specs,
            scratch_shapes=[pltpu.VMEM((n_tile_slots + 1, part, TW), F32)],
        ),
        out_shape=out_shape,
        name=f"gather{chunk}",
    )(table, *args)


def final_kernel(prior_ref, red_ref, *refs):
    out_ref = refs[-1]
    for s in range(red_ref.shape[0]):
        cols = slice(s * TW, (s + 1) * TW)
        out_ref[:, :, cols] = prior_ref[:, :, cols] + red_ref[s].astype(F32)


def final(chunk, prior, red, out):
    begin, part = sum(PARTS[:chunk]), PARTS[chunk]
    step = 16
    n_row, _, width = prior.shape
    per = red.shape[0]
    spec = pl.BlockSpec((n_row, step, width), lambda i: (0, begin // step + i, 0))
    args, in_specs, alias = [prior, red], [spec], {}
    in_specs.append(pl.BlockSpec((per, n_row, step, TW), lambda i: (0, 0, i, 0)))
    if out is not None:
        args.append(out)
        in_specs.append(pl.BlockSpec(memory_space=pl.ANY))
        alias = {2: 0}
    return pl.pallas_call(
        final_kernel,
        grid=(part // step,),
        in_specs=in_specs,
        out_specs=spec,
        out_shape=jax.ShapeDtypeStruct(prior.shape, F32),
        input_output_aliases=alias,
        name=f"final{chunk}",
    )(*args)


def on_device(design, observed, obs_type, owner_of, sub_of, sigma_table, solution, prior):
    n_owner = lax.axis_size("tile")
    n_arc = lax.axis_size("arc")
    blocks = design.shape[0]
    per_owner = solution.shape[0] // TW
    tile_count = per_owner * n_owner
    row_tiles = tile_count // n_arc
    own_index = lax.axis_index("tile")

    tile_ids = (owner_of * per_owner + sub_of).reshape(blocks * 4)
    small = jnp.concatenate([solution, tile_ids.astype(F32)])
    small = jnp.pad(small, (0, 4 * TW - small.shape[0])).reshape(1, 4, TW)
    small = jnp.broadcast_to(small, (n_owner, 4, TW))
    everyone = lax.all_to_all(small, "tile", split_axis=0, concat_axis=0, tiled=True)
    sol = everyone[:, :per_owner].reshape(tile_count, TW)
    all_ids = everyone[:, per_owner, : blocks * 4].astype(jnp.int32)

    wt, head = weigh(tile_ids, sigma_table, design, observed, obs_type, sol)
    owners = owner_of.reshape(-1)

    def exchange(chunk):
        p = pack(chunk, owners, wt, head, n_owner)
        p = p.reshape(n_owner, SLOTS, *p.shape[1:])
        return p

    def send(p):
        g = lax.all_to_all(p, "tile", split_axis=0, concat_axis=0, tiled=True)
        return g.reshape(n_owner * SLOTS, *p.shape[2:])

    spare = tile_count * per_owner
    hit = (all_ids // per_owner == own_index).astype(jnp.int32)
    items = blocks * 4
    lower = (jnp.arange(items)[:, None] < jnp.arange(items)[None, :]).astype(jnp.int32)
    rank = jnp.sum(hit[:, :, None] * lower[None], axis=1)
    pick = hit[:, None, :] * (rank[:, None, :] == jnp.arange(SLOTS)[None, :, None]).astype(
        jnp.int32
    )
    dead = 1 - jnp.sum(pick, axis=2)
    sub = all_ids % per_owner
    grid = all_ids.reshape(n_owner, blocks, 4)
    columns = [jnp.sum(pick * sub[:, None, :], axis=2) + dead * per_owner]
    for r in range(4):
        ids = jnp.roll(grid, -r, axis=2).reshape(n_owner, items)
        place = (
            (ids // row_tiles) * (per_owner * row_tiles) + sub * row_tiles + ids % row_tiles
        )
        columns.append(jnp.sum(pick * place[:, None, :], axis=2) + dead * spare)
    table = jnp.stack(columns, axis=2).reshape(-1)

    got, reds = [], []
    payload = exchange(0)
    got.append(send(payload))
    payload = exchange(1)
    panel, = gather(0, table, got, spare)
    panel, payload = lax.optimization_barrier((panel, payload))
    panel = panel.reshape(n_arc, per_owner, row_tiles, PARTS[0], TW)
    reds.append(lax.psum_scatter(panel, "arc", scatter_dimension=0, tiled=True)[0])
    got.append(send(payload))
    panel, grad = gather(1, table, got, spare)
    panel = panel.reshape(n_arc, per_owner, row_tiles, PARTS[1], TW)
    reds.append(lax.psum_scatter(panel, "arc", scatter_dimension=0, tiled=True)[0])
    gradient = lax.psum(grad[:per_owner].reshape(-1), "arc")

    prior = prior.reshape(row_tiles, TW, per_owner * TW)
    out = final(0, prior, reds[0], None)
    out = final(1, prior, reds[1], out)
    return out.reshape(row_tiles * TW, per_owner * TW), gradient


def solution(mesh):
    both = ("arc", "tile")
    in_specs = (
        P(both, None, None),
        P(both, None),
        P(both, None),
        P(both, None),
        P(both, None),
        P(),
        P("tile"),
        P("arc", "tile"),
    )
    return jax.shard_map(
        on_device,
        mesh=mesh,
        in_specs=in_specs,
        out_specs=(P("arc", "tile"), P("tile")),
        check_vma=False,
    )
```

```python
import functools

import jax
import jax.numpy as jnp
from jax import lax
from jax.experimental import pallas as pl
from jax.experimental.pallas import tpu as pltpu
from jax.sharding import PartitionSpec as P


HUBER = 1.345
TW = 128
SLOTS = 2
HEAD = 16
PARTS = (48, 80)
UNROLL = 8
BATCH = 6
F32 = jnp.float32
BF16 = jnp.bfloat16
NT = (((1,), (1,)), ((), ()))


def prepare_kernel(owner_ref, design_ref, dt_ref, table_ref):
    blocks = design_ref.shape[0]

    @pl.loop(0, table_ref.shape[0])
    def _(i):
        table_ref[i] = -1

    @pl.loop(0, blocks * 4)
    def _(i):
        first = owner_ref[i] * SLOTS
        table_ref[jnp.where(table_ref[first] < 0, first, first + 1)] = i

    for b in range(blocks):
        for l in range(4):
            dt_ref[b * 4 + l] = design_ref[b, :, l * TW : (l + 1) * TW].T


def prepare(owner, design, n_owner):
    blocks = design.shape[0]
    vmem = pl.BlockSpec(memory_space=pltpu.VMEM)
    smem = pl.BlockSpec(memory_space=pltpu.SMEM)
    return pl.pallas_call(
        prepare_kernel,
        in_specs=[smem, vmem],
        out_specs=[vmem, smem],
        out_shape=[
            jax.ShapeDtypeStruct((blocks * 4, TW, TW), BF16),
            jax.ShapeDtypeStruct((n_owner * SLOTS,), jnp.int32),
        ],
        name="prepare",
    )(owner, design)


def weigh(ids_ref, sigma_ref, dt_ref, observed_ref, type_ref, sol_ref, wt_ref, head_ref):
    blocks = observed_ref.shape[0]
    head_ref[...] = jnp.zeros_like(head_ref)
    spread = jnp.zeros(observed_ref.shape, F32)
    for k in range(sigma_ref.shape[0]):
        spread = jnp.where(type_ref[...] == k, sigma_ref[k], spread)
    row = lax.broadcasted_iota(jnp.int32, (8, TW), 0)
    for b in range(blocks):
        predicted = jnp.zeros((8, TW), F32)
        for l in range(4):
            s = jnp.broadcast_to(sol_ref[pl.ds(ids_ref[b * 4 + l], 1), :], (8, TW))
            hi = s.astype(BF16).astype(F32)
            mid = (s - hi).astype(BF16).astype(F32)
            low = s - hi - mid
            terms = jnp.where(row == 0, hi, jnp.where(row == 1, mid, low))
            terms = jnp.where(row < 3, terms, 0.0).astype(BF16)
            predicted += jnp.dot(terms, dt_ref[b * 4 + l], preferred_element_type=F32)
        predicted = jnp.sum(predicted, axis=0, keepdims=True)
        residual = observed_ref[b : b + 1] - predicted
        spr = spread[b : b + 1]
        scaled = jnp.abs(residual) / spr
        root = jnp.sqrt(HUBER / jnp.maximum(scaled, HUBER)) / spr
        head_ref[b, 0:1, :] = (root * residual).astype(BF16)
        for l in range(4):
            wt_ref[b * 4 + l] = (root * dt_ref[b * 4 + l].astype(F32)).astype(BF16)


def pack_kernel(chunk, table_ref, *refs):
    if chunk == 0:
        wt_ref, head_ref, out_ref = refs[-3:]

        @pl.when(pl.program_id(0) == 0)
        def _():
            weigh(*refs[:-1])

    else:
        wt_ref, head_ref, out_ref = refs
    step = pl.program_id(0)
    group = out_ref.shape[0]
    begin, part = sum(PARTS[:chunk]), PARTS[chunk]

    for g in range(group):
        item = table_ref[step * group + g]

        @pl.when(item >= 0)
        def _():
            b = item // 4
            m = item - b * 4
            base = 0
            if chunk == 0:
                out_ref[g, 0:TW, :] = wt_ref[item]
                base = TW
            if chunk == len(PARTS) - 1:
                out_ref[g, base : base + HEAD, :] = head_ref[b]
                base += HEAD
            for r in range(3):
                other = b * 4 + lax.rem(m + r + 1, 4)
                out_ref[g, base : base + part, :] = wt_ref[other, begin : begin + part, :]
                base += part


def payload_rows(chunk):
    rows = 3 * PARTS[chunk]
    return rows + TW * (chunk == 0) + HEAD * (chunk == len(PARTS) - 1)


def pack(chunk, table, *args):
    n_slot = table.shape[0]
    group = 8
    rows = payload_rows(chunk)
    whole = lambda x: pl.BlockSpec(x.shape, lambda i, *_: (0,) * len(x.shape))
    out_specs = [pl.BlockSpec((group, rows, TW), lambda i, *_: (i, 0, 0))]
    out_shape = [jax.ShapeDtypeStruct((n_slot, rows, TW), BF16)]
    if chunk == 0:
        dt, observed = args[2], args[3]
        kept = [
            jax.ShapeDtypeStruct(dt.shape, BF16),
            jax.ShapeDtypeStruct((observed.shape[0], HEAD, TW), BF16),
        ]
        smem = pl.BlockSpec(memory_space=pltpu.SMEM)
        in_specs = [smem, smem] + [whole(x) for x in args[2:]]
        out_specs = [whole(x) for x in kept] + out_specs
        out_shape = kept + out_shape
    else:
        in_specs = [whole(x) for x in args]
    return pl.pallas_call(
        functools.partial(pack_kernel, chunk),
        grid_spec=pltpu.PrefetchScalarGridSpec(
            num_scalar_prefetch=1,
            grid=(n_slot // group,),
            in_specs=in_specs,
            out_specs=out_specs,
        ),
        out_shape=out_shape,
    )(table, *args)


def gather_kernel(chunk, table_ref, *refs):
    last = chunk == len(PARTS) - 1
    main_ref = refs[0]
    side_ref = refs[0] if chunk == 0 else refs[1]
    panel_ref = refs[1 if chunk == 0 else 2]
    grad_ref = refs[-4] if last else None
    acc_ref, cast_ref, sems = refs[-3:]
    group = main_ref.shape[0]
    begin, part = sum(PARTS[:chunk]), PARTS[chunk]
    skip = HEAD if last else 0
    top = TW if chunk == 0 else 0
    step = pl.program_id(0)

    @pl.when(step == 0)
    def _():
        if last:
            grad_ref[...] = jnp.zeros_like(grad_ref)

        @pl.loop(0, cast_ref.shape[0] // BATCH)
        def _(i):
            for k in range(BATCH):
                acc_ref[i * BATCH + k] = jnp.zeros(acc_ref.shape[1:], F32)

    for g0 in range(0, group, UNROLL):
        prods = []
        for g in range(g0, g0 + UNROLL):
            own = main_ref[g, 0:TW, :]
            side = side_ref[g, top : top + skip + 3 * part, :]
            diag = main_ref[g, begin : begin + part, :]
            prods.append(
                [
                    lax.dot_general(x, own, NT, preferred_element_type=F32)
                    for x in (side, diag)
                ]
            )
        for u, (side, diag) in enumerate(prods):
            item = (step * group + g0 + u) * 5
            acc_ref[table_ref[item + 1]] += diag
            for r in range(3):
                acc_ref[table_ref[item + 2 + r]] += side[
                    skip + r * part : skip + (r + 1) * part
                ]
            if last:
                grad_ref[pl.ds(table_ref[item], 1), :] += side[0:1]

    @pl.when(step == pl.num_programs(0) - 1)
    def _():
        pieces = sems.shape[0]
        piece = cast_ref.shape[0] // pieces
        copies = []
        for p in range(pieces):

            @pl.loop(0, piece // BATCH)
            def _(i):
                for k in range(BATCH):
                    at = p * piece + i * BATCH + k
                    cast_ref[at] = acc_ref[at].astype(BF16)

            rows = pl.ds(p * piece, piece)
            copies.append(
                pltpu.make_async_copy(cast_ref.at[rows], panel_ref.at[rows], sems.at[p])
            )
            copies[-1].start()
        for copy in copies:
            copy.wait()


def gather(chunk, table, got, n_tile_slots):
    part = PARTS[chunk]
    group = 8
    n_slot = got[0].shape[0]
    main_rows = got[0].shape[1] if chunk == 0 else TW
    in_specs = [pl.BlockSpec((group, main_rows, TW), lambda i, *_: (i, 0, 0))]
    args = [got[0]]
    out_specs = [pl.BlockSpec(memory_space=pltpu.HBM)]
    out_shape = [jax.ShapeDtypeStruct((n_tile_slots, part, TW), BF16)]
    if chunk > 0:
        in_specs.append(
            pl.BlockSpec((group, payload_rows(chunk), TW), lambda i, *_: (i, 0, 0))
        )
        args.append(got[chunk])
    if chunk == len(PARTS) - 1:
        out_specs.append(pl.BlockSpec((8, TW), lambda i, *_: (0, 0)))
        out_shape.append(jax.ShapeDtypeStruct((8, TW), F32))
    return pl.pallas_call(
        functools.partial(gather_kernel, chunk),
        grid_spec=pltpu.PrefetchScalarGridSpec(
            num_scalar_prefetch=1,
            grid=(n_slot // group,),
            in_specs=in_specs,
            out_specs=out_specs,
            scratch_shapes=[
                pltpu.VMEM((n_tile_slots + 1, part, TW), F32),
                pltpu.VMEM((n_tile_slots, part, TW), BF16),
                pltpu.SemaphoreType.DMA((4,)),
            ],
        ),
        out_shape=out_shape,
    )(table, *args)


def final_kernel(prior_ref, red_ref, *refs):
    out_ref = refs[-1]
    for s in range(red_ref.shape[0]):
        cols = slice(s * TW, (s + 1) * TW)
        out_ref[:, :, cols] = prior_ref[:, :, cols] + red_ref[s].astype(F32)


def final(chunk, prior, red, out):
    begin, part = sum(PARTS[:chunk]), PARTS[chunk]
    step = 16
    n_row, _, width = prior.shape
    per = red.shape[0]
    spec = pl.BlockSpec((n_row, step, width), lambda i: (0, begin // step + i, 0))
    args, in_specs, alias = [prior, red], [spec], {}
    in_specs.append(pl.BlockSpec((per, n_row, step, TW), lambda i: (0, 0, i, 0)))
    if out is not None:
        args.append(out)
        in_specs.append(pl.BlockSpec(memory_space=pl.ANY))
        alias = {2: 0}
    return pl.pallas_call(
        final_kernel,
        grid=(part // step,),
        in_specs=in_specs,
        out_specs=spec,
        out_shape=jax.ShapeDtypeStruct(prior.shape, F32),
        input_output_aliases=alias,
    )(*args)


def on_device(design, observed, obs_type, owner_of, sub_of, sigma_table, solution, prior):
    n_owner = lax.axis_size("tile")
    n_arc = lax.axis_size("arc")
    blocks = design.shape[0]
    per_owner = solution.shape[0] // TW
    tile_count = per_owner * n_owner
    row_tiles = tile_count // n_arc
    own_index = lax.axis_index("tile")

    tile_ids = (owner_of * per_owner + sub_of).reshape(blocks * 4)
    small = jnp.concatenate([solution, tile_ids.astype(F32)])
    small = jnp.pad(small, (0, 4 * TW - small.shape[0])).reshape(1, 4, TW)
    small = jnp.broadcast_to(small, (n_owner, 4, TW))
    everyone = lax.all_to_all(small, "tile", split_axis=0, concat_axis=0, tiled=True)
    sol = everyone[:, :per_owner].reshape(tile_count, TW)
    all_ids = everyone[:, per_owner, : blocks * 4].astype(jnp.int32)

    dt, slots = prepare(owner_of.reshape(-1), design, n_owner)
    wt, head, payload = pack(
        0, slots, tile_ids, sigma_table, dt, observed, obs_type, sol
    )

    def send(p):
        p = p.reshape(n_owner, SLOTS, *p.shape[1:])
        g = lax.all_to_all(p, "tile", split_axis=0, concat_axis=0, tiled=True)
        return g.reshape(n_owner * SLOTS, *p.shape[2:])

    spare = tile_count * per_owner
    hit = (all_ids // per_owner == own_index).astype(jnp.int32)
    items = blocks * 4
    lower = (jnp.arange(items)[:, None] < jnp.arange(items)[None, :]).astype(jnp.int32)
    rank = jnp.sum(hit[:, :, None] * lower[None], axis=1)
    pick = hit[:, None, :] * (rank[:, None, :] == jnp.arange(SLOTS)[None, :, None]).astype(
        jnp.int32
    )
    dead = 1 - jnp.sum(pick, axis=2)
    sub = all_ids % per_owner
    grid = all_ids.reshape(n_owner, blocks, 4)
    columns = [jnp.sum(pick * sub[:, None, :], axis=2) + dead * per_owner]
    for r in range(4):
        ids = jnp.roll(grid, -r, axis=2).reshape(n_owner, items)
        place = (
            (ids // row_tiles) * (per_owner * row_tiles) + sub * row_tiles + ids % row_tiles
        )
        columns.append(jnp.sum(pick * place[:, None, :], axis=2) + dead * spare)
    table = jnp.stack(columns, axis=2).reshape(-1)

    got, reds = [], []
    first = send(payload)
    (payload,) = pack(1, slots, wt, head)
    first, payload = lax.optimization_barrier((first, payload))
    got.append(first)
    (panel,) = gather(0, table, got, spare)
    panel = panel.reshape(n_arc, per_owner, row_tiles, PARTS[0], TW)
    reds.append(lax.psum_scatter(panel, "arc", scatter_dimension=0, tiled=True)[0])
    got.append(send(payload))
    panel, grad = gather(1, table, got, spare)
    panel = panel.reshape(n_arc, per_owner, row_tiles, PARTS[1], TW)
    reds.append(lax.psum_scatter(panel, "arc", scatter_dimension=0, tiled=True)[0])
    gradient = lax.psum(grad[:per_owner].reshape(-1), "arc")

    prior = prior.reshape(row_tiles, TW, per_owner * TW)
    out = final(0, prior, reds[0], None)
    out = final(1, prior, reds[1], out)
    return out.reshape(row_tiles * TW, per_owner * TW), gradient


def solution(mesh):
    both = ("arc", "tile")
    in_specs = (
        P(both, None, None),
        P(both, None),
        P(both, None),
        P(both, None),
        P(both, None),
        P(),
        P("tile"),
        P("arc", "tile"),
    )
    return jax.shard_map(
        on_device,
        mesh=mesh,
        in_specs=in_specs,
        out_specs=(P("arc", "tile"), P("tile")),
        check_vma=False,
    )
```

```python
import functools

import jax
import jax.numpy as jnp
from jax import lax
from jax.experimental import pallas as pl
from jax.experimental.pallas import tpu as pltpu
from jax.sharding import PartitionSpec as P


HUBER = 1.345
TW = 128
SLOTS = 2
HEAD = 16
PARTS = (48, 80)
UNROLL = 8
BATCH = 6
ENTRY = 8
F32 = jnp.float32
BF16 = jnp.bfloat16
NT = (((1,), (1,)), ((), ()))


def prepare_kernel(owner_ref, design_ref, dt_ref, table_ref):
    blocks = design_ref.shape[0]

    @pl.loop(0, table_ref.shape[0])
    def _(i):
        table_ref[i] = -1

    @pl.loop(0, blocks * 4)
    def _(i):
        first = owner_ref[i] * SLOTS
        table_ref[jnp.where(table_ref[first] < 0, first, first + 1)] = i

    for b in range(blocks):
        for l in range(4):
            dt_ref[b * 4 + l] = design_ref[b, :, l * TW : (l + 1) * TW].T


def prepare(owner, design, n_owner):
    blocks = design.shape[0]
    vmem = pl.BlockSpec(memory_space=pltpu.VMEM)
    smem = pl.BlockSpec(memory_space=pltpu.SMEM)
    return pl.pallas_call(
        prepare_kernel,
        in_specs=[smem, vmem],
        out_specs=[vmem, smem],
        out_shape=[
            jax.ShapeDtypeStruct((blocks * 4, TW, TW), BF16),
            jax.ShapeDtypeStruct((n_owner * SLOTS,), jnp.int32),
        ],
        name="prepare",
    )(owner, design)


def weigh(ids_ref, sigma_ref, dt_ref, observed_ref, type_ref, sol_ref, wt_ref, head_ref):
    blocks = observed_ref.shape[0]
    head_ref[...] = jnp.zeros_like(head_ref)
    spread = jnp.zeros(observed_ref.shape, F32)
    for k in range(sigma_ref.shape[0]):
        spread = jnp.where(type_ref[...] == k, sigma_ref[k], spread)
    row = lax.broadcasted_iota(jnp.int32, (8, TW), 0)
    for b in range(blocks):
        predicted = jnp.zeros((8, TW), F32)
        for l in range(4):
            s = jnp.broadcast_to(sol_ref[pl.ds(ids_ref[b * 4 + l], 1), :], (8, TW))
            hi = s.astype(BF16).astype(F32)
            mid = (s - hi).astype(BF16).astype(F32)
            low = s - hi - mid
            terms = jnp.where(row == 0, hi, jnp.where(row == 1, mid, low))
            terms = jnp.where(row < 3, terms, 0.0).astype(BF16)
            predicted += jnp.dot(terms, dt_ref[b * 4 + l], preferred_element_type=F32)
        predicted = jnp.sum(predicted, axis=0, keepdims=True)
        residual = observed_ref[b : b + 1] - predicted
        spr = spread[b : b + 1]
        scaled = jnp.abs(residual) / spr
        root = jnp.sqrt(HUBER / jnp.maximum(scaled, HUBER)) / spr
        head_ref[b, 0:1, :] = (root * residual).astype(BF16)
        for l in range(4):
            wt_ref[b * 4 + l] = (root * dt_ref[b * 4 + l].astype(F32)).astype(BF16)


def pack_kernel(chunk, table_ref, *refs):
    if chunk == 0:
        wt_ref, head_ref, out_ref = refs[-3:]

        @pl.when(pl.program_id(0) == 0)
        def _():
            weigh(*refs[:-1])

    else:
        wt_ref, head_ref, out_ref = refs
    step = pl.program_id(0)
    group = out_ref.shape[0]
    begin, part = sum(PARTS[:chunk]), PARTS[chunk]

    for g in range(group):
        item = table_ref[step * group + g]

        @pl.when(item >= 0)
        def _():
            b = item // 4
            m = item - b * 4
            base = 0
            if chunk == 0:
                out_ref[g, 0:TW, :] = wt_ref[item]
                base = TW
            if chunk == len(PARTS) - 1:
                out_ref[g, base : base + HEAD, :] = head_ref[b]
                base += HEAD
            for r in range(3):
                other = b * 4 + lax.rem(m + r + 1, 4)
                out_ref[g, base : base + part, :] = wt_ref[other, begin : begin + part, :]
                base += part


def payload_rows(chunk):
    rows = 3 * PARTS[chunk]
    return rows + TW * (chunk == 0) + HEAD * (chunk == len(PARTS) - 1)


def pack(chunk, table, *args):
    n_slot = table.shape[0]
    group = 8
    rows = payload_rows(chunk)
    whole = lambda x: pl.BlockSpec(x.shape, lambda i, *_: (0,) * len(x.shape))
    out_specs = [pl.BlockSpec((group, rows, TW), lambda i, *_: (i, 0, 0))]
    out_shape = [jax.ShapeDtypeStruct((n_slot, rows, TW), BF16)]
    if chunk == 0:
        dt, observed = args[2], args[3]
        kept = [
            jax.ShapeDtypeStruct(dt.shape, BF16),
            jax.ShapeDtypeStruct((observed.shape[0], HEAD, TW), BF16),
        ]
        smem = pl.BlockSpec(memory_space=pltpu.SMEM)
        in_specs = [smem, smem] + [whole(x) for x in args[2:]]
        out_specs = [whole(x) for x in kept] + out_specs
        out_shape = kept + out_shape
    else:
        in_specs = [whole(x) for x in args]
    return pl.pallas_call(
        functools.partial(pack_kernel, chunk),
        grid_spec=pltpu.PrefetchScalarGridSpec(
            num_scalar_prefetch=1,
            grid=(n_slot // group,),
            in_specs=in_specs,
            out_specs=out_specs,
        ),
        out_shape=out_shape,
    )(table, *args)


def route_kernel(per_owner, n_arc, row_tiles, items, where_ref, all_ref, out_ref):
    ids = all_ref[:, per_owner, :].astype(jnp.int32)
    lane = lax.broadcasted_iota(jnp.int32, ids.shape, 1)
    own, arc = where_ref[0], where_ref[1]
    first = own * per_owner
    sub = ids - first
    hit = (sub >= 0) & (sub < per_owner) & (lane < items)
    taken = hit.astype(F32)
    k = lax.broadcasted_iota(jnp.int32, (TW, TW), 0)
    upper = (k < lax.broadcasted_iota(jnp.int32, (TW, TW), 1)).astype(F32)
    rank = jnp.dot(taken, upper, preferred_element_type=F32)
    half = row_tiles // 2
    columns = [sub]
    for r in range(4):
        ahead = pltpu.roll(ids, TW - r, 1) if r else ids
        behind = pltpu.roll(ids, 4 - r, 1) if r else ids
        tile = jnp.where(lane % 4 + r < 4, ahead, behind)
        high = jnp.zeros_like(tile)
        for a in range(1, n_arc):
            high += (tile >= a * row_tiles).astype(jnp.int32)
        row = tile - high * row_tiles
        side = (row >= half).astype(jnp.int32)
        distance = high - arc
        distance = jnp.where(distance < 0, distance + n_arc, distance)
        columns.append(((distance * 2 + side) * per_owner + sub) * half + row - side * half)
    dead = [per_owner] + [n_arc * row_tiles * per_owner] * 4
    out = jnp.zeros(out_ref.shape, F32)
    at = lax.broadcasted_iota(jnp.int32, out_ref.shape, 1)
    for slot in range(SLOTS):
        pick = jnp.where(rank == slot, taken, 0.0)
        live = jnp.sum(pick, axis=1, keepdims=True)
        for c, column in enumerate(columns):
            value = jnp.sum(pick * column.astype(F32), axis=1, keepdims=True)
            value += (1.0 - live) * dead[c]
            out = jnp.where(at == slot * ENTRY + c, value, out)
    out_ref[...] = out.astype(jnp.int32)


def route(where, everyone, per_owner, n_arc, row_tiles, items):
    n_owner = everyone.shape[0]
    vmem = pl.BlockSpec(memory_space=pltpu.VMEM)
    return pl.pallas_call(
        functools.partial(route_kernel, per_owner, n_arc, row_tiles, items),
        in_specs=[pl.BlockSpec(memory_space=pltpu.SMEM), vmem],
        out_specs=vmem,
        out_shape=jax.ShapeDtypeStruct((n_owner, SLOTS * ENTRY), jnp.int32),
        name="route",
    )(where, everyone)


def gather_kernel(chunk, table_ref, *refs):
    last = chunk == len(PARTS) - 1
    main_ref = refs[0]
    side_ref = refs[0] if chunk == 0 else refs[1]
    panel_ref, up_ref, down_ref = refs[1 if chunk == 0 else 2 :][:3]
    grad_ref = refs[-4] if last else None
    acc_ref, cast_ref, sems = refs[-3:]
    group = main_ref.shape[0]
    begin, part = sum(PARTS[:chunk]), PARTS[chunk]
    skip = HEAD if last else 0
    top = TW if chunk == 0 else 0
    step = pl.program_id(0)

    @pl.when(step == 0)
    def _():
        if last:
            grad_ref[...] = jnp.zeros_like(grad_ref)

        @pl.loop(0, cast_ref.shape[0] // BATCH)
        def _(i):
            for k in range(BATCH):
                acc_ref[i * BATCH + k] = jnp.zeros(acc_ref.shape[1:], F32)

    for g0 in range(0, group, UNROLL):
        prods = []
        for g in range(g0, g0 + UNROLL):
            own = main_ref[g, 0:TW, :]
            side = side_ref[g, top : top + skip + 3 * part, :]
            diag = main_ref[g, begin : begin + part, :]
            prods.append(
                [
                    lax.dot_general(x, own, NT, preferred_element_type=F32)
                    for x in (side, diag)
                ]
            )
        for u, (side, diag) in enumerate(prods):
            item = (step * group + g0 + u) * ENTRY
            acc_ref[table_ref[item + 1]] += diag
            for r in range(3):
                acc_ref[table_ref[item + 2 + r]] += side[
                    skip + r * part : skip + (r + 1) * part
                ]
            if last:
                grad_ref[pl.ds(table_ref[item], 1), :] += side[0:1]

    @pl.when(step == pl.num_programs(0) - 1)
    def _():
        n_arc = sems.shape[0] - 1
        piece = cast_ref.shape[0] // n_arc
        half = piece // 2
        copies = []
        for n, p in enumerate([n_arc // 2] + [p for p in range(n_arc) if p != n_arc // 2]):

            @pl.loop(0, piece // BATCH)
            def _(i):
                for k in range(BATCH):
                    at = p * piece + i * BATCH + k
                    cast_ref[at] = acc_ref[at].astype(BF16)

            if n == 0:
                moves = [
                    (pl.ds(p * piece, half), up_ref, n_arc),
                    (pl.ds(p * piece + half, half), down_ref, p),
                ]
            else:
                rows = pl.ds(p * piece, piece)
                moves = [(rows, panel_ref.at[rows], p)]
            for rows, target, sem in moves:
                copies.append(pltpu.make_async_copy(cast_ref.at[rows], target, sems.at[sem]))
                copies[-1].start()
        for copy in copies:
            copy.wait()


def gather(chunk, table, got, n_tile_slots, n_arc):
    part = PARTS[chunk]
    group = 8
    n_slot = got[0].shape[0]
    main_rows = got[0].shape[1] if chunk == 0 else TW
    in_specs = [pl.BlockSpec((group, main_rows, TW), lambda i, *_: (i, 0, 0))]
    args = [got[0]]
    out_specs = [pl.BlockSpec(memory_space=pltpu.HBM)] * 3
    half = n_tile_slots // n_arc // 2
    out_shape = [
        jax.ShapeDtypeStruct((n, part, TW), BF16) for n in (n_tile_slots, half, half)
    ]
    if chunk > 0:
        in_specs.append(
            pl.BlockSpec((group, payload_rows(chunk), TW), lambda i, *_: (i, 0, 0))
        )
        args.append(got[chunk])
    if chunk == len(PARTS) - 1:
        out_specs.append(pl.BlockSpec((8, TW), lambda i, *_: (0, 0)))
        out_shape.append(jax.ShapeDtypeStruct((8, TW), F32))
    return pl.pallas_call(
        functools.partial(gather_kernel, chunk),
        grid_spec=pltpu.PrefetchScalarGridSpec(
            num_scalar_prefetch=1,
            grid=(n_slot // group,),
            in_specs=in_specs,
            out_specs=out_specs,
            scratch_shapes=[
                pltpu.VMEM((n_tile_slots + 1, part, TW), F32),
                pltpu.VMEM((n_tile_slots, part, TW), BF16),
                pltpu.SemaphoreType.DMA((n_arc + 1,)),
            ],
        ),
        out_shape=out_shape,
    )(table, *args)


def final_kernel(prior_ref, own_ref, up_ref, down_ref, *refs):
    out_ref = refs[-1]
    n_row, _, width = prior_ref.shape
    per = width // TW
    half = n_row // 2
    for h in range(2):
        for s in range(per):
            rows = slice(h * half, (h + 1) * half)
            cols = slice(s * TW, (s + 1) * TW)
            tiles = slice((h * per + s) * half, (h * per + s + 1) * half)
            out_ref[rows, :, cols] = (
                prior_ref[rows, :, cols]
                + own_ref[tiles].astype(F32)
                + up_ref[tiles].astype(F32)
                + down_ref[tiles].astype(F32)
            )


def final(chunk, prior, panel, up, down, out):
    begin, part = sum(PARTS[:chunk]), PARTS[chunk]
    step = 16
    n_row, _, width = prior.shape
    per = up.shape[0]
    spec = pl.BlockSpec((n_row, step, width), lambda i: (0, begin // step + i, 0))
    tiles = pl.BlockSpec((per, step, TW), lambda i: (0, i, 0))
    args, in_specs, alias = [prior, panel, up, down], [spec] + [tiles] * 3, {}
    if out is not None:
        args.append(out)
        in_specs.append(pl.BlockSpec(memory_space=pl.ANY))
        alias = {4: 0}
    return pl.pallas_call(
        final_kernel,
        grid=(part // step,),
        in_specs=in_specs,
        out_specs=spec,
        out_shape=jax.ShapeDtypeStruct(prior.shape, F32),
        input_output_aliases=alias,
    )(*args)


def ring(panel, up, down, grad, n_arc):
    piece = panel.shape[0] // n_arc
    half = piece // 2
    far = n_arc // 2
    rising = [(i, (i + 1) % n_arc) for i in range(n_arc)]
    falling = [((i + 1) % n_arc, i) for i in range(n_arc)]
    own = lambda p, a, b: panel[p * piece + a : p * piece + b]
    add = lambda x, y: (x.astype(F32) + y.astype(F32)).astype(BF16)
    for s in range(far):
        if s == 1:
            up = jnp.concatenate([add(own(far - 1, 0, half), up), own(far - 1, half, piece)])
            down = jnp.concatenate(
                [own(far + 1, 0, half), add(own(far + 1, half, piece), down)]
            )
        elif s > 1:
            up = add(own(far - s, 0, piece), up)
            down = add(own(far + s, 0, piece), down)
        if grad is None:
            up, down = lax.optimization_barrier((up, down))
        else:
            up, down, grad = lax.optimization_barrier((up, down, grad))
        up = lax.ppermute(up, "arc", rising)
        down = lax.ppermute(down, "arc", falling)
        if grad is None:
            up, down = lax.optimization_barrier((up, down))
        else:
            other = grad
            if 1 << s < n_arc:
                swap = [(i, i ^ (1 << s)) for i in range(n_arc)]
                other = lax.ppermute(grad, "arc", swap)
            up, down, other = lax.optimization_barrier((up, down, other))
            if 1 << s < n_arc:
                grad = grad + other
    return up, down, grad


def on_device(design, observed, obs_type, owner_of, sub_of, sigma_table, solution, prior):
    n_owner = lax.axis_size("tile")
    n_arc = lax.axis_size("arc")
    blocks = design.shape[0]
    per_owner = solution.shape[0] // TW
    tile_count = per_owner * n_owner
    row_tiles = tile_count // n_arc
    own_index = lax.axis_index("tile")
    arc_index = lax.axis_index("arc")

    tile_ids = (owner_of * per_owner + sub_of).reshape(blocks * 4)
    small = jnp.concatenate([solution, tile_ids.astype(F32)])
    small = jnp.pad(small, (0, 4 * TW - small.shape[0])).reshape(1, 4, TW)
    small = jnp.broadcast_to(small, (n_owner, 4, TW))
    everyone = lax.all_to_all(small, "tile", split_axis=0, concat_axis=0, tiled=True)
    sol = everyone[:, :per_owner].reshape(tile_count, TW)

    dt, slots = prepare(owner_of.reshape(-1), design, n_owner)
    wt, head, payload = pack(
        0, slots, tile_ids, sigma_table, dt, observed, obs_type, sol
    )

    def send(p):
        p = p.reshape(n_owner, SLOTS, *p.shape[1:])
        g = lax.all_to_all(p, "tile", split_axis=0, concat_axis=0, tiled=True)
        return g.reshape(n_owner * SLOTS, *p.shape[2:])

    spare = tile_count * per_owner
    where = jnp.stack([own_index, arc_index]).astype(jnp.int32)
    table = route(where, everyone, per_owner, n_arc, row_tiles, blocks * 4).reshape(-1)

    got = []
    first = send(payload)
    (payload,) = pack(1, slots, wt, head)
    first, payload, table = lax.optimization_barrier((first, payload, table))
    got.append(first)
    panel0, up, down = gather(0, table, got, spare, n_arc)
    got.append(send(payload))
    up0, down0, _ = ring(panel0, up, down, None, n_arc)
    panel1, up, down, grad = gather(1, table, got, spare, n_arc)
    up1, down1, grad = ring(panel1, up, down, grad, n_arc)
    gradient = grad[:per_owner].reshape(-1)

    prior = prior.reshape(row_tiles, TW, per_owner * TW)
    out = final(0, prior, panel0, up0, down0, None)
    out = final(1, prior, panel1, up1, down1, out)
    return out.reshape(row_tiles * TW, per_owner * TW), gradient


def solution(mesh):
    both = ("arc", "tile")
    in_specs = (
        P(both, None, None),
        P(both, None),
        P(both, None),
        P(both, None),
        P(both, None),
        P(),
        P("tile"),
        P("arc", "tile"),
    )
    return jax.shard_map(
        on_device,
        mesh=mesh,
        in_specs=in_specs,
        out_specs=(P("arc", "tile"), P("tile")),
        check_vma=False,
    )
```

```python
import functools

import jax
import jax.numpy as jnp
from jax import lax
from jax.experimental import pallas as pl
from jax.experimental.pallas import tpu as pltpu
from jax.sharding import PartitionSpec as P


HUBER = 1.345
TW = 128
SLOTS = 2
HEAD = 16
PARTS = (64, 64)
UNROLL = 8
BATCH = 6
ENTRY = 8
F32 = jnp.float32
BF16 = jnp.bfloat16
NT = (((1,), (1,)), ((), ()))


def prepare_kernel(owner_ref, design_ref, dt_ref, table_ref):
    blocks = design_ref.shape[0]

    @pl.loop(0, table_ref.shape[0])
    def _(i):
        table_ref[i] = -1

    @pl.loop(0, blocks * 4)
    def _(i):
        first = owner_ref[i] * SLOTS
        table_ref[jnp.where(table_ref[first] < 0, first, first + 1)] = i

    for b in range(blocks):
        for l in range(4):
            dt_ref[b * 4 + l] = design_ref[b, :, l * TW : (l + 1) * TW].T


def prepare(owner, design, n_owner):
    blocks = design.shape[0]
    vmem = pl.BlockSpec(memory_space=pltpu.VMEM)
    smem = pl.BlockSpec(memory_space=pltpu.SMEM)
    return pl.pallas_call(
        prepare_kernel,
        in_specs=[smem, vmem],
        out_specs=[vmem, smem],
        out_shape=[
            jax.ShapeDtypeStruct((blocks * 4, TW, TW), BF16),
            jax.ShapeDtypeStruct((n_owner * SLOTS,), jnp.int32),
        ],
        name="prepare",
    )(owner, design)


def weigh(ids_ref, sigma_ref, dt_ref, observed_ref, type_ref, sol_ref, wt_ref, head_ref):
    blocks = observed_ref.shape[0]
    head_ref[...] = jnp.zeros_like(head_ref)
    spread = jnp.zeros(observed_ref.shape, F32)
    for k in range(sigma_ref.shape[0]):
        spread = jnp.where(type_ref[...] == k, sigma_ref[k], spread)
    row = lax.broadcasted_iota(jnp.int32, (8, TW), 0)
    for b in range(blocks):
        predicted = jnp.zeros((8, TW), F32)
        for l in range(4):
            s = jnp.broadcast_to(sol_ref[pl.ds(ids_ref[b * 4 + l], 1), :], (8, TW))
            hi = s.astype(BF16).astype(F32)
            mid = (s - hi).astype(BF16).astype(F32)
            low = s - hi - mid
            terms = jnp.where(row == 0, hi, jnp.where(row == 1, mid, low))
            terms = jnp.where(row < 3, terms, 0.0).astype(BF16)
            predicted += jnp.dot(terms, dt_ref[b * 4 + l], preferred_element_type=F32)
        predicted = jnp.sum(predicted, axis=0, keepdims=True)
        residual = observed_ref[b : b + 1] - predicted
        spr = spread[b : b + 1]
        scaled = jnp.abs(residual) / spr
        root = jnp.sqrt(HUBER / jnp.maximum(scaled, HUBER)) / spr
        head_ref[b, 0:1, :] = (root * residual).astype(BF16)
        for l in range(4):
            wt_ref[b * 4 + l] = (root * dt_ref[b * 4 + l].astype(F32)).astype(BF16)


def pack_kernel(chunk, table_ref, *refs):
    if chunk == 0:
        wt_ref, head_ref, out_ref = refs[-3:]

        @pl.when(pl.program_id(0) == 0)
        def _():
            weigh(*refs[:-1])

    else:
        wt_ref, head_ref, out_ref = refs
    step = pl.program_id(0)
    group = out_ref.shape[0]
    begin, part = sum(PARTS[:chunk]), PARTS[chunk]

    for g in range(group):
        item = table_ref[step * group + g]

        @pl.when(item >= 0)
        def _():
            b = item // 4
            m = item - b * 4
            base = 0
            if chunk == 0:
                out_ref[g, 0:TW, :] = wt_ref[item]
                base = TW
            if chunk == len(PARTS) - 1:
                out_ref[g, base : base + HEAD, :] = head_ref[b]
                base += HEAD
            for r in range(3):
                other = b * 4 + lax.rem(m + r + 1, 4)
                out_ref[g, base : base + part, :] = wt_ref[other, begin : begin + part, :]
                base += part


def payload_rows(chunk):
    rows = 3 * PARTS[chunk]
    return rows + TW * (chunk == 0) + HEAD * (chunk == len(PARTS) - 1)


def pack(chunk, table, *args):
    n_slot = table.shape[0]
    group = 8
    rows = payload_rows(chunk)
    whole = lambda x: pl.BlockSpec(x.shape, lambda i, *_: (0,) * len(x.shape))
    out_specs = [pl.BlockSpec((group, rows, TW), lambda i, *_: (i, 0, 0))]
    out_shape = [jax.ShapeDtypeStruct((n_slot, rows, TW), BF16)]
    if chunk == 0:
        dt, observed = args[2], args[3]
        kept = [
            jax.ShapeDtypeStruct(dt.shape, BF16),
            jax.ShapeDtypeStruct((observed.shape[0], HEAD, TW), BF16),
        ]
        smem = pl.BlockSpec(memory_space=pltpu.SMEM)
        in_specs = [smem, smem] + [whole(x) for x in args[2:]]
        out_specs = [whole(x) for x in kept] + out_specs
        out_shape = kept + out_shape
    else:
        in_specs = [whole(x) for x in args]
    return pl.pallas_call(
        functools.partial(pack_kernel, chunk),
        grid_spec=pltpu.PrefetchScalarGridSpec(
            num_scalar_prefetch=1,
            grid=(n_slot // group,),
            in_specs=in_specs,
            out_specs=out_specs,
        ),
        out_shape=out_shape,
    )(table, *args)


def route_kernel(per_owner, n_arc, row_tiles, items, where_ref, all_ref, out_ref):
    ids = all_ref[:, per_owner, :].astype(jnp.int32)
    lane = lax.broadcasted_iota(jnp.int32, ids.shape, 1)
    own, arc = where_ref[0], where_ref[1]
    first = own * per_owner
    sub = ids - first
    hit = (sub >= 0) & (sub < per_owner) & (lane < items)
    taken = hit.astype(F32)
    k = lax.broadcasted_iota(jnp.int32, (TW, TW), 0)
    upper = (k < lax.broadcasted_iota(jnp.int32, (TW, TW), 1)).astype(F32)
    rank = jnp.dot(taken, upper, preferred_element_type=F32)
    half = row_tiles // 2
    columns = [sub]
    for r in range(4):
        ahead = pltpu.roll(ids, TW - r, 1) if r else ids
        behind = pltpu.roll(ids, 4 - r, 1) if r else ids
        tile = jnp.where(lane % 4 + r < 4, ahead, behind)
        high = jnp.zeros_like(tile)
        for a in range(1, n_arc):
            high += (tile >= a * row_tiles).astype(jnp.int32)
        row = tile - high * row_tiles
        side = (row >= half).astype(jnp.int32)
        distance = high - arc
        distance = jnp.where(distance < 0, distance + n_arc, distance)
        columns.append(((distance * 2 + side) * per_owner + sub) * half + row - side * half)
    dead = [per_owner] + [n_arc * row_tiles * per_owner] * 4
    out = jnp.zeros(out_ref.shape, F32)
    at = lax.broadcasted_iota(jnp.int32, out_ref.shape, 1)
    for slot in range(SLOTS):
        pick = jnp.where(rank == slot, taken, 0.0)
        live = jnp.sum(pick, axis=1, keepdims=True)
        for c, column in enumerate(columns):
            value = jnp.sum(pick * column.astype(F32), axis=1, keepdims=True)
            value += (1.0 - live) * dead[c]
            out = jnp.where(at == slot * ENTRY + c, value, out)
    out_ref[...] = out.astype(jnp.int32)


def route(where, everyone, per_owner, n_arc, row_tiles, items):
    n_owner = everyone.shape[0]
    vmem = pl.BlockSpec(memory_space=pltpu.VMEM)
    return pl.pallas_call(
        functools.partial(route_kernel, per_owner, n_arc, row_tiles, items),
        in_specs=[pl.BlockSpec(memory_space=pltpu.SMEM), vmem],
        out_specs=vmem,
        out_shape=jax.ShapeDtypeStruct((n_owner, SLOTS * ENTRY), jnp.int32),
        name="route",
    )(where, everyone)


def gather_kernel(chunk, table_ref, *refs):
    last = chunk == len(PARTS) - 1
    main_ref = refs[0]
    side_ref = refs[0] if chunk == 0 else refs[1]
    panels, firsts = refs[1 if chunk == 0 else 2 :][:2], refs[1 if chunk == 0 else 2 :][2:6]
    grad_ref = refs[-4] if last else None
    acc_ref, cast_ref, sems = refs[-3:]
    group = main_ref.shape[0]
    begin, part = sum(PARTS[:chunk]), PARTS[chunk]
    skip = HEAD if last else 0
    top = TW if chunk == 0 else 0
    step = pl.program_id(0)

    @pl.when(step == 0)
    def _():
        if last:
            grad_ref[...] = jnp.zeros_like(grad_ref)

        @pl.loop(0, cast_ref.shape[0] // BATCH)
        def _(i):
            for k in range(BATCH):
                acc_ref[i * BATCH + k] = jnp.zeros(acc_ref.shape[1:], F32)

    for g0 in range(0, group, UNROLL):
        prods = []
        for g in range(g0, g0 + UNROLL):
            own = main_ref[g, 0:TW, :]
            side = side_ref[g, top : top + skip + 3 * part, :]
            diag = main_ref[g, begin : begin + part, :]
            prods.append(
                [
                    lax.dot_general(x, own, NT, preferred_element_type=F32)
                    for x in (side, diag)
                ]
            )
        for u, (side, diag) in enumerate(prods):
            item = (step * group + g0 + u) * ENTRY
            acc_ref[table_ref[item + 1]] += diag
            for r in range(3):
                acc_ref[table_ref[item + 2 + r]] += side[
                    skip + r * part : skip + (r + 1) * part
                ]
            if last:
                grad_ref[pl.ds(table_ref[item], 1), :] += side[0:1]

    @pl.when(step == pl.num_programs(0) - 1)
    def _():
        n_arc = sems.shape[0] // 2
        far = n_arc // 2
        piece = cast_ref.shape[0] // n_arc
        half = piece // 2
        alone = {(far, 0): 0, (far, 1): 1, (far + 1, 0): 2, (far - 1, 1): 3}
        near = [far, far + 1, far - 1]
        copies = []
        for p in near + [p for p in range(n_arc) if p not in near]:

            @pl.loop(0, piece // BATCH)
            def _(i):
                for k in range(BATCH):
                    at = p * piece + i * BATCH + k
                    cast_ref[at] = acc_ref[at].astype(BF16)

            for h in range(2):
                rows = pl.ds(p * piece + h * half, half)
                target = panels[h].at[pl.ds(p * half, half)]
                if (p, h) in alone:
                    target = firsts[alone[p, h]]
                copies.append(
                    pltpu.make_async_copy(cast_ref.at[rows], target, sems.at[2 * p + h])
                )
                copies[-1].start()
        for copy in copies:
            copy.wait()


def gather(chunk, table, got, n_tile_slots, n_arc):
    part = PARTS[chunk]
    group = 8
    n_slot = got[0].shape[0]
    main_rows = got[0].shape[1] if chunk == 0 else TW
    in_specs = [pl.BlockSpec((group, main_rows, TW), lambda i, *_: (i, 0, 0))]
    args = [got[0]]
    out_specs = [pl.BlockSpec(memory_space=pltpu.HBM)] * 6
    half = n_tile_slots // n_arc // 2
    out_shape = [
        jax.ShapeDtypeStruct((n, part, TW), BF16) for n in [half * n_arc] * 2 + [half] * 4
    ]
    if chunk > 0:
        in_specs.append(
            pl.BlockSpec((group, payload_rows(chunk), TW), lambda i, *_: (i, 0, 0))
        )
        args.append(got[chunk])
    if chunk == len(PARTS) - 1:
        out_specs.append(pl.BlockSpec((8, TW), lambda i, *_: (0, 0)))
        out_shape.append(jax.ShapeDtypeStruct((8, TW), F32))
    return pl.pallas_call(
        functools.partial(gather_kernel, chunk),
        grid_spec=pltpu.PrefetchScalarGridSpec(
            num_scalar_prefetch=1,
            grid=(n_slot // group,),
            in_specs=in_specs,
            out_specs=out_specs,
            scratch_shapes=[
                pltpu.VMEM((n_tile_slots + 1, part, TW), F32),
                pltpu.VMEM((n_tile_slots, part, TW), BF16),
                pltpu.SemaphoreType.DMA((2 * n_arc,)),
            ],
        ),
        out_shape=out_shape,
    )(table, *args)


def final_kernel(prior_ref, *refs):
    out_ref = refs[-1]
    n_row, _, width = prior_ref.shape
    per = width // TW
    half = n_row // 2
    for h in range(2):
        own_ref, up_ref, down_ref = refs[3 * h : 3 * h + 3]
        for s in range(per):
            rows = slice(h * half, (h + 1) * half)
            cols = slice(s * TW, (s + 1) * TW)
            tiles = slice(s * half, (s + 1) * half)
            out_ref[rows, :, cols] = (
                prior_ref[rows, :, cols]
                + own_ref[tiles].astype(F32)
                + up_ref[tiles].astype(F32)
                + down_ref[tiles].astype(F32)
            )


def final(chunk, prior, sums, out):
    begin, part = sum(PARTS[:chunk]), PARTS[chunk]
    step = 16
    n_row, _, width = prior.shape
    per = sums[1].shape[0]
    spec = pl.BlockSpec((n_row, step, width), lambda i: (0, begin // step + i, 0))
    tiles = pl.BlockSpec((per, step, TW), lambda i: (0, i, 0))
    args, alias = [prior, *sums], {}
    in_specs = [spec] + [tiles] * 6
    if out is not None:
        args.append(out)
        in_specs.append(pl.BlockSpec(memory_space=pl.ANY))
        alias = {len(args) - 1: 0}
    return pl.pallas_call(
        final_kernel,
        grid=(part // step,),
        in_specs=in_specs,
        out_specs=spec,
        out_shape=jax.ShapeDtypeStruct(prior.shape, F32),
        input_output_aliases=alias,
    )(*args)


def ring(panels, firsts, grad, n_arc):
    half = panels[0].shape[0] // n_arc
    far = n_arc // 2
    rising = [(i, (i + 1) % n_arc) for i in range(n_arc)]
    falling = [((i + 1) % n_arc, i) for i in range(n_arc)]
    add = lambda x, y: (x.astype(F32) + y.astype(F32)).astype(BF16)
    state = [[firsts[0], None], [None, firsts[1]]]
    for s in range(far):
        for h in range(2):
            up, down = state[h]
            own = lambda p: panels[h][p * half : (p + 1) * half]
            if s > h:
                up = add(own(far - s), up)
            elif s == 1:
                up = firsts[3]
            if s > 1 - h:
                down = add(own(far + s), down)
            elif s == 1:
                down = firsts[2]
            paired = h == 0 and grad is not None and 1 << s < n_arc
            extra = [grad] if paired else []
            up, down, *extra = lax.optimization_barrier((up, down, *extra))
            if up is not None:
                up = lax.ppermute(up, "arc", rising)
            if down is not None:
                down = lax.ppermute(down, "arc", falling)
            if paired:
                swap = [(i, i ^ (1 << s)) for i in range(n_arc)]
                extra = [lax.ppermute(extra[0], "arc", swap)]
            up, down, *extra = lax.optimization_barrier((up, down, *extra))
            if paired:
                grad = grad + extra[0]
            state[h] = [up, down]
    return [panels[0], *state[0], panels[1], *state[1]], grad


def on_device(design, observed, obs_type, owner_of, sub_of, sigma_table, solution, prior):
    n_owner = lax.axis_size("tile")
    n_arc = lax.axis_size("arc")
    blocks = design.shape[0]
    per_owner = solution.shape[0] // TW
    tile_count = per_owner * n_owner
    row_tiles = tile_count // n_arc
    own_index = lax.axis_index("tile")
    arc_index = lax.axis_index("arc")

    tile_ids = (owner_of * per_owner + sub_of).reshape(blocks * 4)
    small = jnp.concatenate([solution, tile_ids.astype(F32)])
    small = jnp.pad(small, (0, 4 * TW - small.shape[0])).reshape(1, 4, TW)
    small = jnp.broadcast_to(small, (n_owner, 4, TW))
    everyone = lax.all_to_all(small, "tile", split_axis=0, concat_axis=0, tiled=True)
    sol = everyone[:, :per_owner].reshape(tile_count, TW)

    dt, slots = prepare(owner_of.reshape(-1), design, n_owner)
    wt, head, payload = pack(
        0, slots, tile_ids, sigma_table, dt, observed, obs_type, sol
    )

    def send(p):
        p = p.reshape(n_owner, SLOTS, *p.shape[1:])
        g = lax.all_to_all(p, "tile", split_axis=0, concat_axis=0, tiled=True)
        return g.reshape(n_owner * SLOTS, *p.shape[2:])

    spare = tile_count * per_owner
    where = jnp.stack([own_index, arc_index]).astype(jnp.int32)
    table = route(where, everyone, per_owner, n_arc, row_tiles, blocks * 4).reshape(-1)

    got = []
    first = send(payload)
    (payload,) = pack(1, slots, wt, head)
    first, payload, table = lax.optimization_barrier((first, payload, table))
    got.append(first)
    outs = gather(0, table, got, spare, n_arc)
    got.append(send(payload))
    sums0, _ = ring(outs[:2], outs[2:6], None, n_arc)
    *outs, grad = gather(1, table, got, spare, n_arc)
    sums1, grad = ring(outs[:2], outs[2:6], grad, n_arc)
    gradient = grad[:per_owner].reshape(-1)

    prior = prior.reshape(row_tiles, TW, per_owner * TW)
    out = final(0, prior, sums0, None)
    out = final(1, prior, sums1, out)
    return out.reshape(row_tiles * TW, per_owner * TW), gradient


def solution(mesh):
    both = ("arc", "tile")
    in_specs = (
        P(both, None, None),
        P(both, None),
        P(both, None),
        P(both, None),
        P(both, None),
        P(),
        P("tile"),
        P("arc", "tile"),
    )
    return jax.shard_map(
        on_device,
        mesh=mesh,
        in_specs=in_specs,
        out_specs=(P("arc", "tile"), P("tile")),
        check_vma=False,
    )
```

```python
import functools

import jax
import jax.numpy as jnp
from jax import lax
from jax.experimental import pallas as pl
from jax.experimental.pallas import tpu as pltpu
from jax.sharding import PartitionSpec as P


HUBER = 1.345
TW = 128
SLOTS = 2
HEAD = 16
PARTS = (64, 64)
UNROLL = 8
BATCH = 6
ENTRY = 8
F32 = jnp.float32
BF16 = jnp.bfloat16
NT = (((1,), (1,)), ((), ()))


def prepare_kernel(owner_ref, design_ref, dt_ref, table_ref):
    blocks = design_ref.shape[0]

    @pl.loop(0, table_ref.shape[0])
    def _(i):
        table_ref[i] = -1

    @pl.loop(0, blocks * 4)
    def _(i):
        first = owner_ref[i] * SLOTS
        table_ref[jnp.where(table_ref[first] < 0, first, first + 1)] = i

    for b in range(blocks):
        for l in range(4):
            dt_ref[b * 4 + l] = design_ref[b, :, l * TW : (l + 1) * TW].T


def prepare(owner, design, n_owner):
    blocks = design.shape[0]
    vmem = pl.BlockSpec(memory_space=pltpu.VMEM)
    smem = pl.BlockSpec(memory_space=pltpu.SMEM)
    return pl.pallas_call(
        prepare_kernel,
        in_specs=[smem, vmem],
        out_specs=[vmem, smem],
        out_shape=[
            jax.ShapeDtypeStruct((blocks * 4, TW, TW), BF16),
            jax.ShapeDtypeStruct((n_owner * SLOTS,), jnp.int32),
        ],
        name="prepare",
    )(owner, design)


def weigh(ids_ref, sigma_ref, dt_ref, observed_ref, type_ref, sol_ref, wt_ref, head_ref):
    blocks = observed_ref.shape[0]
    head_ref[...] = jnp.zeros_like(head_ref)
    spread = jnp.zeros(observed_ref.shape, F32)
    for k in range(sigma_ref.shape[0]):
        spread = jnp.where(type_ref[...] == k, sigma_ref[k], spread)
    row = lax.broadcasted_iota(jnp.int32, (8, TW), 0)
    line = lax.broadcasted_iota(jnp.int32, (blocks, TW), 0)
    predicted = jnp.zeros((blocks, TW), F32)
    for b in range(blocks):
        parts = []
        for l in range(4):
            s = jnp.broadcast_to(sol_ref[pl.ds(ids_ref[b * 4 + l], 1), :], (8, TW))
            hi = s.astype(BF16).astype(F32)
            mid = (s - hi).astype(BF16).astype(F32)
            low = s - hi - mid
            terms = jnp.where(row == 0, hi, jnp.where(row == 1, mid, low))
            terms = jnp.where(row < 3, terms, 0.0).astype(BF16)
            parts.append(jnp.dot(terms, dt_ref[b * 4 + l], preferred_element_type=F32))
        total = (parts[0] + parts[1]) + (parts[2] + parts[3])
        total = jnp.sum(total, axis=0, keepdims=True)
        predicted = jnp.where(line == b, total, predicted)
    residual = observed_ref[...] - predicted
    scaled = jnp.abs(residual) / spread
    root = jnp.sqrt(HUBER / jnp.maximum(scaled, HUBER)) / spread
    target = root * residual
    for b in range(blocks):
        head_ref[b, 0:1, :] = target[b : b + 1].astype(BF16)
        for l in range(4):
            tile = dt_ref[b * 4 + l].astype(F32)
            wt_ref[b * 4 + l] = (root[b : b + 1] * tile).astype(BF16)


def pack_kernel(chunk, table_ref, *refs):
    if chunk == 0:
        wt_ref, head_ref, out_ref = refs[-3:]

        @pl.when(pl.program_id(0) == 0)
        def _():
            weigh(*refs[:-1])

    else:
        wt_ref, head_ref, out_ref = refs
    step = pl.program_id(0)
    group = out_ref.shape[0]
    begin, part = sum(PARTS[:chunk]), PARTS[chunk]

    for g in range(group):
        item = table_ref[step * group + g]

        @pl.when(item >= 0)
        def _():
            b = item // 4
            m = item - b * 4
            base = 0
            if chunk == 0:
                out_ref[g, 0:TW, :] = wt_ref[item]
                base = TW
            if chunk == len(PARTS) - 1:
                out_ref[g, base : base + HEAD, :] = head_ref[b]
                base += HEAD
            for r in range(3):
                other = b * 4 + lax.rem(m + r + 1, 4)
                out_ref[g, base : base + part, :] = wt_ref[other, begin : begin + part, :]
                base += part


def payload_rows(chunk):
    rows = 3 * PARTS[chunk]
    return rows + TW * (chunk == 0) + HEAD * (chunk == len(PARTS) - 1)


def pack(chunk, table, *args):
    n_slot = table.shape[0]
    group = 16
    rows = payload_rows(chunk)
    whole = lambda x: pl.BlockSpec(x.shape, lambda i, *_: (0,) * len(x.shape))
    out_specs = [pl.BlockSpec((group, rows, TW), lambda i, *_: (i, 0, 0))]
    out_shape = [jax.ShapeDtypeStruct((n_slot, rows, TW), BF16)]
    if chunk == 0:
        dt, observed = args[2], args[3]
        kept = [
            jax.ShapeDtypeStruct(dt.shape, BF16),
            jax.ShapeDtypeStruct((observed.shape[0], HEAD, TW), BF16),
        ]
        smem = pl.BlockSpec(memory_space=pltpu.SMEM)
        in_specs = [smem, smem] + [whole(x) for x in args[2:]]
        out_specs = [whole(x) for x in kept] + out_specs
        out_shape = kept + out_shape
    else:
        in_specs = [whole(x) for x in args]
    return pl.pallas_call(
        functools.partial(pack_kernel, chunk),
        grid_spec=pltpu.PrefetchScalarGridSpec(
            num_scalar_prefetch=1,
            grid=(n_slot // group,),
            in_specs=in_specs,
            out_specs=out_specs,
        ),
        out_shape=out_shape,
    )(table, *args)


def route_kernel(per_owner, n_arc, row_tiles, items, where_ref, all_ref, out_ref):
    ids = all_ref[:, per_owner, :].astype(jnp.int32)
    lane = lax.broadcasted_iota(jnp.int32, ids.shape, 1)
    own, arc = where_ref[0], where_ref[1]
    first = own * per_owner
    sub = ids - first
    hit = (sub >= 0) & (sub < per_owner) & (lane < items)
    taken = hit.astype(F32)
    k = lax.broadcasted_iota(jnp.int32, (TW, TW), 0)
    upper = (k < lax.broadcasted_iota(jnp.int32, (TW, TW), 1)).astype(F32)
    rank = jnp.dot(taken, upper, preferred_element_type=F32)
    half = row_tiles // 2
    columns = [sub]
    for r in range(4):
        ahead = pltpu.roll(ids, TW - r, 1) if r else ids
        behind = pltpu.roll(ids, 4 - r, 1) if r else ids
        tile = jnp.where(lane % 4 + r < 4, ahead, behind)
        high = jnp.zeros_like(tile)
        for a in range(1, n_arc):
            high += (tile >= a * row_tiles).astype(jnp.int32)
        row = tile - high * row_tiles
        side = (row >= half).astype(jnp.int32)
        distance = high - arc
        distance = jnp.where(distance < 0, distance + n_arc, distance)
        columns.append(((distance * 2 + side) * per_owner + sub) * half + row - side * half)
    dead = [per_owner] + [n_arc * row_tiles * per_owner] * 4
    out = jnp.zeros(out_ref.shape, F32)
    at = lax.broadcasted_iota(jnp.int32, out_ref.shape, 1)
    for slot in range(SLOTS):
        pick = jnp.where(rank == slot, taken, 0.0)
        live = jnp.sum(pick, axis=1, keepdims=True)
        for c, column in enumerate(columns):
            value = jnp.sum(pick * column.astype(F32), axis=1, keepdims=True)
            value += (1.0 - live) * dead[c]
            out = jnp.where(at == slot * ENTRY + c, value, out)
    out_ref[...] = out.astype(jnp.int32)


def route(where, everyone, per_owner, n_arc, row_tiles, items):
    n_owner = everyone.shape[0]
    vmem = pl.BlockSpec(memory_space=pltpu.VMEM)
    return pl.pallas_call(
        functools.partial(route_kernel, per_owner, n_arc, row_tiles, items),
        in_specs=[pl.BlockSpec(memory_space=pltpu.SMEM), vmem],
        out_specs=vmem,
        out_shape=jax.ShapeDtypeStruct((n_owner, SLOTS * ENTRY), jnp.int32),
        name="route",
    )(where, everyone)


def gather_kernel(chunk, table_ref, *refs):
    last = chunk == len(PARTS) - 1
    main_ref = refs[0]
    side_ref = refs[0] if chunk == 0 else refs[1]
    panels, firsts = refs[1 if chunk == 0 else 2 :][:2], refs[1 if chunk == 0 else 2 :][2:6]
    grad_ref = refs[-4] if last else None
    acc_ref, cast_ref, sems = refs[-3:]
    group = main_ref.shape[0]
    begin, part = sum(PARTS[:chunk]), PARTS[chunk]
    skip = HEAD if last else 0
    top = TW if chunk == 0 else 0
    step = pl.program_id(0)

    @pl.when(step == 0)
    def _():
        if last:
            grad_ref[...] = jnp.zeros_like(grad_ref)

        @pl.loop(0, cast_ref.shape[0] // BATCH)
        def _(i):
            for k in range(BATCH):
                acc_ref[i * BATCH + k] = jnp.zeros(acc_ref.shape[1:], F32)

    @pl.loop(0, group // UNROLL)
    def _(batch):
        prods = []
        for u in range(UNROLL):
            g = batch * UNROLL + u
            own = main_ref[g, 0:TW, :]
            at = g if chunk == 0 else step * group + g
            side = side_ref[at, top : top + skip + 3 * part, :]
            diag = main_ref[g, begin : begin + part, :]
            prods.append(
                [
                    lax.dot_general(x, own, NT, preferred_element_type=F32)
                    for x in (side, diag)
                ]
            )
        for u, (side, diag) in enumerate(prods):
            item = (step * group + batch * UNROLL + u) * ENTRY
            acc_ref[table_ref[item + 1]] += diag
            for r in range(3):
                acc_ref[table_ref[item + 2 + r]] += side[
                    skip + r * part : skip + (r + 1) * part
                ]
            if last:
                grad_ref[pl.ds(table_ref[item], 1), :] += side[0:1]

    @pl.when(step == pl.num_programs(0) - 1)
    def _():
        n_arc = sems.shape[0] // 2
        far = n_arc // 2
        piece = cast_ref.shape[0] // n_arc
        half = piece // 2
        alone = {(far, 0): 0, (far, 1): 1, (far + 1, 0): 2, (far - 1, 1): 3}
        near = [far, far + 1, far - 1]
        copies = []
        for p in near + [p for p in range(n_arc) if p not in near]:

            @pl.loop(0, piece // BATCH)
            def _(i):
                for k in range(BATCH):
                    at = p * piece + i * BATCH + k
                    cast_ref[at] = acc_ref[at].astype(BF16)

            for h in range(2):
                rows = pl.ds(p * piece + h * half, half)
                target = panels[h].at[pl.ds(p * half, half)]
                if (p, h) in alone:
                    target = firsts[alone[p, h]]
                copies.append(
                    pltpu.make_async_copy(cast_ref.at[rows], target, sems.at[2 * p + h])
                )
                copies[-1].start()
        for copy in copies:
            copy.wait()


def gather(chunk, table, got, n_tile_slots, n_arc):
    part = PARTS[chunk]
    group = 16
    n_slot = got[0].shape[0]
    main_rows = got[0].shape[1] if chunk == 0 else TW
    in_specs = [pl.BlockSpec((group, main_rows, TW), lambda i, *_: (i, 0, 0))]
    args = [got[0]]
    out_specs = [pl.BlockSpec(memory_space=pltpu.HBM)] * 6
    half = n_tile_slots // n_arc // 2
    out_shape = [
        jax.ShapeDtypeStruct((n, part, TW), BF16) for n in [half * n_arc] * 2 + [half] * 4
    ]
    if chunk > 0:
        in_specs.append(pl.BlockSpec(memory_space=pltpu.VMEM))
        args.append(pltpu.with_memory_space_constraint(got[chunk], pltpu.VMEM))
    if chunk == len(PARTS) - 1:
        out_specs.append(pl.BlockSpec((8, TW), lambda i, *_: (0, 0)))
        out_shape.append(jax.ShapeDtypeStruct((8, TW), F32))
    return pl.pallas_call(
        functools.partial(gather_kernel, chunk),
        grid_spec=pltpu.PrefetchScalarGridSpec(
            num_scalar_prefetch=1,
            grid=(n_slot // group,),
            in_specs=in_specs,
            out_specs=out_specs,
            scratch_shapes=[
                pltpu.VMEM((n_tile_slots + 1, part, TW), F32),
                pltpu.VMEM((n_tile_slots, part, TW), BF16),
                pltpu.SemaphoreType.DMA((2 * n_arc,)),
            ],
        ),
        out_shape=out_shape,
    )(table, *args)


def final_kernel(prior_ref, *refs):
    out_ref = refs[-1]
    n_row, step, width = prior_ref.shape
    per = width // TW
    half = n_row // 2
    at = pl.ds(pl.multiple_of(pl.program_id(0) * step, step), step)
    for h in range(2):
        own_ref, up_ref, down_ref = refs[3 * h : 3 * h + 3]
        for s in range(per):
            rows = slice(h * half, (h + 1) * half)
            cols = slice(s * TW, (s + 1) * TW)
            tiles = slice(s * half, (s + 1) * half)
            out_ref[rows, :, cols] = (
                prior_ref[rows, :, cols]
                + own_ref[tiles].astype(F32)
                + up_ref[tiles, at, :].astype(F32)
                + down_ref[tiles, at, :].astype(F32)
            )


def final(chunk, prior, sums, out):
    begin, part = sum(PARTS[:chunk]), PARTS[chunk]
    step = 16
    n_row, _, width = prior.shape
    per = sums[1].shape[0]
    spec = pl.BlockSpec((n_row, step, width), lambda i: (0, begin // step + i, 0))
    tiles = pl.BlockSpec((per, step, TW), lambda i: (0, i, 0))
    kept = pl.BlockSpec(memory_space=pltpu.VMEM)
    if out is not None:
        sums = [
            x if i % 3 == 0 else pltpu.with_memory_space_constraint(x, pltpu.VMEM)
            for i, x in enumerate(sums)
        ]
    args, alias = [prior, *sums], {}
    in_specs = [spec] + [tiles, kept, kept] * 2
    if out is not None:
        args.append(out)
        in_specs.append(pl.BlockSpec(memory_space=pl.ANY))
        alias = {len(args) - 1: 0}
    return pl.pallas_call(
        final_kernel,
        grid=(part // step,),
        in_specs=in_specs,
        out_specs=spec,
        out_shape=jax.ShapeDtypeStruct(prior.shape, F32),
        input_output_aliases=alias,
    )(*args)


def ring(panels, firsts, grad, n_arc):
    half = panels[0].shape[0] // n_arc
    far = n_arc // 2
    rising = [(i, (i + 1) % n_arc) for i in range(n_arc)]
    falling = [((i + 1) % n_arc, i) for i in range(n_arc)]
    add = lambda x, y: (x.astype(F32) + y.astype(F32)).astype(BF16)
    state = [[firsts[0], None], [None, firsts[1]]]
    for s in range(far):
        for h in range(2):
            up, down = state[h]
            own = lambda p: panels[h][p * half : (p + 1) * half]
            if s > h:
                up = add(own(far - s), up)
            elif s == 1:
                up = firsts[3]
            if s > 1 - h:
                down = add(own(far + s), down)
            elif s == 1:
                down = firsts[2]
            up, down = lax.optimization_barrier((up, down))
            if up is not None:
                up = lax.ppermute(up, "arc", rising)
            if down is not None:
                down = lax.ppermute(down, "arc", falling)
            up, down = lax.optimization_barrier((up, down))
            state[h] = [up, down]
        if grad is not None and 1 << s < n_arc:
            swap = [(i, i ^ (1 << s)) for i in range(n_arc)]
            grad = grad + lax.ppermute(grad, "arc", swap)
    return [panels[0], *state[0], panels[1], *state[1]], grad


def on_device(design, observed, obs_type, owner_of, sub_of, sigma_table, solution, prior):
    n_owner = lax.axis_size("tile")
    n_arc = lax.axis_size("arc")
    blocks = design.shape[0]
    per_owner = solution.shape[0] // TW
    tile_count = per_owner * n_owner
    row_tiles = tile_count // n_arc
    own_index = lax.axis_index("tile")
    arc_index = lax.axis_index("arc")

    tile_ids = (owner_of * per_owner + sub_of).reshape(blocks * 4)
    small = jnp.concatenate([solution, tile_ids.astype(F32)])
    small = jnp.pad(small, (0, 4 * TW - small.shape[0])).reshape(1, 4, TW)
    small = jnp.broadcast_to(small, (n_owner, 4, TW))
    everyone = lax.all_to_all(small, "tile", split_axis=0, concat_axis=0, tiled=True)
    sol = everyone[:, :per_owner].reshape(tile_count, TW)

    dt, slots = prepare(owner_of.reshape(-1), design, n_owner)
    wt, head, payload = pack(
        0, slots, tile_ids, sigma_table, dt, observed, obs_type, sol
    )

    def send(p):
        p = p.reshape(n_owner, SLOTS, *p.shape[1:])
        g = lax.all_to_all(p, "tile", split_axis=0, concat_axis=0, tiled=True)
        return g.reshape(n_owner * SLOTS, *p.shape[2:])

    spare = tile_count * per_owner
    where = jnp.stack([own_index, arc_index]).astype(jnp.int32)
    table = route(where, everyone, per_owner, n_arc, row_tiles, blocks * 4).reshape(-1)

    got = []
    first = send(payload)
    (payload,) = pack(1, slots, wt, head)
    first, payload, table = lax.optimization_barrier((first, payload, table))
    got.append(first)
    outs = gather(0, table, got, spare, n_arc)
    got.append(send(payload))
    sums0, _ = ring(outs[:2], outs[2:6], None, n_arc)
    *outs, grad = gather(1, table, got, spare, n_arc)
    sums1, grad = ring(outs[:2], outs[2:6], grad, n_arc)
    gradient = grad[:per_owner].reshape(-1)

    prior = prior.reshape(row_tiles, TW, per_owner * TW)
    out = final(0, prior, sums0, None)
    out = final(1, prior, sums1, out)
    return out.reshape(row_tiles * TW, per_owner * TW), gradient


def solution(mesh):
    both = ("arc", "tile")
    in_specs = (
        P(both, None, None),
        P(both, None),
        P(both, None),
        P(both, None),
        P(both, None),
        P(),
        P("tile"),
        P("arc", "tile"),
    )
    return jax.shard_map(
        on_device,
        mesh=mesh,
        in_specs=in_specs,
        out_specs=(P("arc", "tile"), P("tile")),
        check_vma=False,
    )
```

```python
import functools

import jax
import jax.numpy as jnp
from jax import lax
from jax.experimental import pallas as pl
from jax.experimental.pallas import tpu as pltpu
from jax.sharding import PartitionSpec as P


HUBER = 1.345
TW = 128
SLOTS = 2
HEAD = 16
PARTS = (64, 64)
UNROLL = 8
BATCH = 6
ENTRY = 8
F32 = jnp.float32
BF16 = jnp.bfloat16
NT = (((1,), (1,)), ((), ()))


def prepare_kernel(owner_ref, design_ref, dt_ref, table_ref):
    blocks = design_ref.shape[0]

    @pl.loop(0, table_ref.shape[0])
    def _(i):
        table_ref[i] = -1

    @pl.loop(0, blocks * 4)
    def _(i):
        first = owner_ref[i] * SLOTS
        table_ref[jnp.where(table_ref[first] < 0, first, first + 1)] = i

    for b in range(blocks):
        for l in range(4):
            dt_ref[b * 4 + l] = design_ref[b, :, l * TW : (l + 1) * TW].T


def prepare(owner, design, n_owner):
    blocks = design.shape[0]
    vmem = pl.BlockSpec(memory_space=pltpu.VMEM)
    smem = pl.BlockSpec(memory_space=pltpu.SMEM)
    return pl.pallas_call(
        prepare_kernel,
        in_specs=[smem, vmem],
        out_specs=[vmem, smem],
        out_shape=[
            jax.ShapeDtypeStruct((blocks * 4, TW, TW), BF16),
            jax.ShapeDtypeStruct((n_owner * SLOTS,), jnp.int32),
        ],
        name="prepare",
    )(owner, design)


def weigh(ids_ref, sigma_ref, dt_ref, observed_ref, type_ref, sol_ref, wt_ref, head_ref):
    blocks = observed_ref.shape[0]
    head_ref[...] = jnp.zeros_like(head_ref)
    spread = jnp.zeros(observed_ref.shape, F32)
    for k in range(sigma_ref.shape[0]):
        spread = jnp.where(type_ref[...] == k, sigma_ref[k], spread)
    row = lax.broadcasted_iota(jnp.int32, (8, TW), 0)
    line = lax.broadcasted_iota(jnp.int32, (blocks, TW), 0)
    predicted = jnp.zeros((blocks, TW), F32)
    for b in range(blocks):
        parts = []
        for l in range(4):
            s = jnp.broadcast_to(sol_ref[pl.ds(ids_ref[b * 4 + l], 1), :], (8, TW))
            hi = s.astype(BF16).astype(F32)
            mid = (s - hi).astype(BF16).astype(F32)
            low = s - hi - mid
            terms = jnp.where(row == 0, hi, jnp.where(row == 1, mid, low))
            terms = jnp.where(row < 3, terms, 0.0).astype(BF16)
            parts.append(jnp.dot(terms, dt_ref[b * 4 + l], preferred_element_type=F32))
        total = (parts[0] + parts[1]) + (parts[2] + parts[3])
        total = jnp.sum(total, axis=0, keepdims=True)
        predicted = jnp.where(line == b, total, predicted)
    residual = observed_ref[...] - predicted
    scaled = jnp.abs(residual) / spread
    root = jnp.sqrt(HUBER / jnp.maximum(scaled, HUBER)) / spread
    target = root * residual
    for b in range(blocks):
        head_ref[b, 0:1, :] = target[b : b + 1].astype(BF16)
        for l in range(4):
            tile = dt_ref[b * 4 + l].astype(F32)
            wt_ref[b * 4 + l] = (root[b : b + 1] * tile).astype(BF16)


def pack_kernel(chunk, table_ref, *refs):
    if chunk == 0:
        wt_ref, head_ref, out_ref = refs[-3:]

        @pl.when(pl.program_id(0) == 0)
        def _():
            weigh(*refs[:-1])

    else:
        wt_ref, head_ref, out_ref = refs
    step = pl.program_id(0)
    group = out_ref.shape[0]
    begin, part = sum(PARTS[:chunk]), PARTS[chunk]

    for g in range(group):
        item = table_ref[step * group + g]

        @pl.when(item >= 0)
        def _():
            b = item // 4
            m = item - b * 4
            base = 0
            if chunk == 0:
                out_ref[g, 0:TW, :] = wt_ref[item]
                base = TW
            if chunk == len(PARTS) - 1:
                out_ref[g, base : base + HEAD, :] = head_ref[b]
                base += HEAD
            for r in range(3):
                other = b * 4 + lax.rem(m + r + 1, 4)
                out_ref[g, base : base + part, :] = wt_ref[other, begin : begin + part, :]
                base += part


def payload_rows(chunk):
    rows = 3 * PARTS[chunk]
    return rows + TW * (chunk == 0) + HEAD * (chunk == len(PARTS) - 1)


def pack(chunk, table, *args):
    n_slot = table.shape[0]
    group = 16
    rows = payload_rows(chunk)
    whole = lambda x: pl.BlockSpec(x.shape, lambda i, *_: (0,) * len(x.shape))
    out_specs = [pl.BlockSpec((group, rows, TW), lambda i, *_: (i, 0, 0))]
    out_shape = [jax.ShapeDtypeStruct((n_slot, rows, TW), BF16)]
    if chunk == 0:
        dt, observed = args[2], args[3]
        kept = [
            jax.ShapeDtypeStruct(dt.shape, BF16),
            jax.ShapeDtypeStruct((observed.shape[0], HEAD, TW), BF16),
        ]
        smem = pl.BlockSpec(memory_space=pltpu.SMEM)
        in_specs = [smem, smem] + [whole(x) for x in args[2:]]
        out_specs = [whole(x) for x in kept] + out_specs
        out_shape = kept + out_shape
    else:
        in_specs = [whole(x) for x in args]
    return pl.pallas_call(
        functools.partial(pack_kernel, chunk),
        grid_spec=pltpu.PrefetchScalarGridSpec(
            num_scalar_prefetch=1,
            grid=(n_slot // group,),
            in_specs=in_specs,
            out_specs=out_specs,
        ),
        out_shape=out_shape,
    )(table, *args)


def route_kernel(per_owner, n_arc, row_tiles, items, where_ref, all_ref, out_ref):
    ids = all_ref[:, per_owner, :].astype(jnp.int32)
    lane = lax.broadcasted_iota(jnp.int32, ids.shape, 1)
    own, arc = where_ref[0], where_ref[1]
    first = own * per_owner
    sub = ids - first
    hit = (sub >= 0) & (sub < per_owner) & (lane < items)
    taken = hit.astype(F32)
    k = lax.broadcasted_iota(jnp.int32, (TW, TW), 0)
    upper = (k < lax.broadcasted_iota(jnp.int32, (TW, TW), 1)).astype(F32)
    rank = jnp.dot(taken, upper, preferred_element_type=F32)
    half = row_tiles // 2
    columns = [sub]
    for r in range(4):
        ahead = pltpu.roll(ids, TW - r, 1) if r else ids
        behind = pltpu.roll(ids, 4 - r, 1) if r else ids
        tile = jnp.where(lane % 4 + r < 4, ahead, behind)
        high = jnp.zeros_like(tile)
        for a in range(1, n_arc):
            high += (tile >= a * row_tiles).astype(jnp.int32)
        row = tile - high * row_tiles
        side = (row >= half).astype(jnp.int32)
        distance = high - arc
        distance = jnp.where(distance < 0, distance + n_arc, distance)
        columns.append(((distance * 2 + side) * per_owner + sub) * half + row - side * half)
    dead = [per_owner] + [n_arc * row_tiles * per_owner] * 4
    out = jnp.zeros(out_ref.shape, F32)
    at = lax.broadcasted_iota(jnp.int32, out_ref.shape, 1)
    for slot in range(SLOTS):
        pick = jnp.where(rank == slot, taken, 0.0)
        live = jnp.sum(pick, axis=1, keepdims=True)
        for c, column in enumerate(columns):
            value = jnp.sum(pick * column.astype(F32), axis=1, keepdims=True)
            value += (1.0 - live) * dead[c]
            out = jnp.where(at == slot * ENTRY + c, value, out)
    out_ref[...] = out.astype(jnp.int32)


def route(where, everyone, per_owner, n_arc, row_tiles, items):
    n_owner = everyone.shape[0]
    vmem = pl.BlockSpec(memory_space=pltpu.VMEM)
    return pl.pallas_call(
        functools.partial(route_kernel, per_owner, n_arc, row_tiles, items),
        in_specs=[pl.BlockSpec(memory_space=pltpu.SMEM), vmem],
        out_specs=vmem,
        out_shape=jax.ShapeDtypeStruct((n_owner, SLOTS * ENTRY), jnp.int32),
        name="route",
    )(where, everyone)


def gather_kernel(chunk, table_ref, *refs):
    last = chunk == len(PARTS) - 1
    main_ref = refs[0]
    side_ref = refs[0] if chunk == 0 else refs[1]
    panels, firsts = refs[1 if chunk == 0 else 2 :][:2], refs[1 if chunk == 0 else 2 :][2:6]
    grad_ref = refs[-4] if last else None
    acc_ref, cast_ref, sems = refs[-3:]
    group = main_ref.shape[0]
    begin, part = sum(PARTS[:chunk]), PARTS[chunk]
    skip = HEAD if last else 0
    top = TW if chunk == 0 else 0
    step = pl.program_id(0)

    @pl.when(step == 0)
    def _():
        if last:
            grad_ref[...] = jnp.zeros_like(grad_ref)

        @pl.loop(0, cast_ref.shape[0] // BATCH)
        def _(i):
            for k in range(BATCH):
                acc_ref[i * BATCH + k] = jnp.zeros(acc_ref.shape[1:], F32)

    @pl.loop(0, group // UNROLL)
    def _(batch):
        prods = []
        for u in range(UNROLL):
            g = batch * UNROLL + u
            own = main_ref[g, 0:TW, :]
            at = g if chunk == 0 else step * group + g
            side = side_ref[at, top : top + skip + 3 * part, :]
            diag = main_ref[g, begin : begin + part, :]
            prods.append(
                [
                    lax.dot_general(x, own, NT, preferred_element_type=F32)
                    for x in (side, diag)
                ]
            )
        for u, (side, diag) in enumerate(prods):
            item = (step * group + batch * UNROLL + u) * ENTRY
            acc_ref[table_ref[item + 1]] += diag
            for r in range(3):
                acc_ref[table_ref[item + 2 + r]] += side[
                    skip + r * part : skip + (r + 1) * part
                ]
            if last:
                grad_ref[pl.ds(table_ref[item], 1), :] += side[0:1]

    @pl.when(step == pl.num_programs(0) - 1)
    def _():
        n_arc = sems.shape[0] // 2
        far = n_arc // 2
        piece = cast_ref.shape[0] // n_arc
        half = piece // 2
        alone = {(far, 0): 0, (far, 1): 1, (far + 1, 0): 2, (far - 1, 1): 3}
        near = [far, far + 1, far - 1]
        copies = []
        for p in near + [p for p in range(n_arc) if p not in near]:

            @pl.loop(0, piece // BATCH)
            def _(i):
                for k in range(BATCH):
                    at = p * piece + i * BATCH + k
                    cast_ref[at] = acc_ref[at].astype(BF16)

            for h in range(2):
                rows = pl.ds(p * piece + h * half, half)
                target = panels[h].at[pl.ds(p * half, half)]
                if (p, h) in alone:
                    target = firsts[alone[p, h]]
                copies.append(
                    pltpu.make_async_copy(cast_ref.at[rows], target, sems.at[2 * p + h])
                )
                copies[-1].start()
        for copy in copies:
            copy.wait()


def gather(chunk, table, got, n_tile_slots, n_arc):
    part = PARTS[chunk]
    group = 16
    n_slot = got[0].shape[0]
    main_rows = got[0].shape[1] if chunk == 0 else TW
    in_specs = [pl.BlockSpec((group, main_rows, TW), lambda i, *_: (i, 0, 0))]
    args = [got[0]]
    out_specs = [pl.BlockSpec(memory_space=pltpu.HBM)] * 6
    half = n_tile_slots // n_arc // 2
    out_shape = [
        jax.ShapeDtypeStruct((n, part, TW), BF16) for n in [half * n_arc] * 2 + [half] * 4
    ]
    if chunk > 0:
        in_specs.append(pl.BlockSpec(memory_space=pltpu.VMEM))
        args.append(pltpu.with_memory_space_constraint(got[chunk], pltpu.VMEM))
    if chunk == len(PARTS) - 1:
        out_specs.append(pl.BlockSpec((8, TW), lambda i, *_: (0, 0)))
        out_shape.append(jax.ShapeDtypeStruct((8, TW), F32))
    return pl.pallas_call(
        functools.partial(gather_kernel, chunk),
        grid_spec=pltpu.PrefetchScalarGridSpec(
            num_scalar_prefetch=1,
            grid=(n_slot // group,),
            in_specs=in_specs,
            out_specs=out_specs,
            scratch_shapes=[
                pltpu.VMEM((n_tile_slots + 1, part, TW), F32),
                pltpu.VMEM((n_tile_slots, part, TW), BF16),
                pltpu.SemaphoreType.DMA((2 * n_arc,)),
            ],
        ),
        out_shape=out_shape,
        compiler_params=pltpu.CompilerParams(
            vmem_limit_bytes=32 << 20
        ),
    )(table, *args)


def final_kernel(prior_ref, *refs):
    out_ref = refs[-1]
    n_row, step, width = prior_ref.shape
    per = width // TW
    half = n_row // 2
    at = pl.ds(pl.multiple_of(pl.program_id(0) * step, step), step)
    for h in range(2):
        own_ref, up_ref, down_ref = refs[3 * h : 3 * h + 3]
        for s in range(per):
            rows = slice(h * half, (h + 1) * half)
            cols = slice(s * TW, (s + 1) * TW)
            tiles = slice(s * half, (s + 1) * half)
            out_ref[rows, :, cols] = (
                prior_ref[rows, :, cols]
                + own_ref[tiles].astype(F32)
                + up_ref[tiles, at, :].astype(F32)
                + down_ref[tiles, at, :].astype(F32)
            )


def final(chunk, prior, sums, out):
    begin, part = sum(PARTS[:chunk]), PARTS[chunk]
    step = 16
    n_row, _, width = prior.shape
    per = sums[1].shape[0]
    spec = pl.BlockSpec((n_row, step, width), lambda i: (0, begin // step + i, 0))
    tiles = pl.BlockSpec((per, step, TW), lambda i: (0, i, 0))
    kept = pl.BlockSpec(memory_space=pltpu.VMEM)
    if out is not None:
        sums = [
            x if i % 3 == 0 else pltpu.with_memory_space_constraint(x, pltpu.VMEM)
            for i, x in enumerate(sums)
        ]
    args, alias = [prior, *sums], {}
    in_specs = [spec] + [tiles, kept, kept] * 2
    if out is not None:
        args.append(out)
        in_specs.append(pl.BlockSpec(memory_space=pl.ANY))
        alias = {len(args) - 1: 0}
    return pl.pallas_call(
        final_kernel,
        grid=(part // step,),
        in_specs=in_specs,
        out_specs=spec,
        out_shape=jax.ShapeDtypeStruct(prior.shape, F32),
        input_output_aliases=alias,
    )(*args)


def ring(panels, firsts, grad, n_arc):
    half = panels[0].shape[0] // n_arc
    far = n_arc // 2
    rising = [(i, (i + 1) % n_arc) for i in range(n_arc)]
    falling = [((i + 1) % n_arc, i) for i in range(n_arc)]
    add = lambda x, y: (x.astype(F32) + y.astype(F32)).astype(BF16)
    state = [[firsts[0], None], [None, firsts[1]]]
    for s in range(far):
        for h in range(2):
            up, down = state[h]
            own = lambda p: panels[h][p * half : (p + 1) * half]
            if s > h:
                up = add(own(far - s), up)
            elif s == 1:
                up = firsts[3]
            if s > 1 - h:
                down = add(own(far + s), down)
            elif s == 1:
                down = firsts[2]
            up, down = lax.optimization_barrier((up, down))
            if up is not None:
                up = lax.ppermute(up, "arc", rising)
            if down is not None:
                down = lax.ppermute(down, "arc", falling)
            up, down = lax.optimization_barrier((up, down))
            state[h] = [up, down]
        if grad is not None and 1 << s < n_arc:
            swap = [(i, i ^ (far >> s)) for i in range(n_arc)]
            grad = grad + lax.ppermute(grad, "arc", swap)
    return [panels[0], *state[0], panels[1], *state[1]], grad


def on_device(design, observed, obs_type, owner_of, sub_of, sigma_table, solution, prior):
    n_owner = lax.axis_size("tile")
    n_arc = lax.axis_size("arc")
    blocks = design.shape[0]
    per_owner = solution.shape[0] // TW
    tile_count = per_owner * n_owner
    row_tiles = tile_count // n_arc
    own_index = lax.axis_index("tile")
    arc_index = lax.axis_index("arc")

    tile_ids = (owner_of * per_owner + sub_of).reshape(blocks * 4)
    small = jnp.concatenate([solution, tile_ids.astype(F32)])
    small = jnp.pad(small, (0, 4 * TW - small.shape[0])).reshape(1, 4, TW)
    small = jnp.broadcast_to(small, (n_owner, 4, TW))
    everyone = lax.all_to_all(small, "tile", split_axis=0, concat_axis=0, tiled=True)
    sol = everyone[:, :per_owner].reshape(tile_count, TW)

    dt, slots = prepare(owner_of.reshape(-1), design, n_owner)
    wt, head, payload = pack(
        0, slots, tile_ids, sigma_table, dt, observed, obs_type, sol
    )

    def send(p):
        p = p.reshape(n_owner, SLOTS, *p.shape[1:])
        g = lax.all_to_all(p, "tile", split_axis=0, concat_axis=0, tiled=True)
        return g.reshape(n_owner * SLOTS, *p.shape[2:])

    spare = tile_count * per_owner
    where = jnp.stack([own_index, arc_index]).astype(jnp.int32)
    table = route(where, everyone, per_owner, n_arc, row_tiles, blocks * 4).reshape(-1)

    got = []
    first = send(payload)
    (payload,) = pack(1, slots, wt, head)
    first, payload, table = lax.optimization_barrier((first, payload, table))
    got.append(first)
    outs = gather(0, table, got, spare, n_arc)
    got.append(send(payload))
    sums0, _ = ring(outs[:2], outs[2:6], None, n_arc)
    *outs, grad = gather(1, table, got, spare, n_arc)
    sums1, grad = ring(outs[:2], outs[2:6], grad, n_arc)
    gradient = grad[:per_owner].reshape(-1)

    prior = prior.reshape(row_tiles, TW, per_owner * TW)
    out = final(0, prior, sums0, None)
    out = final(1, prior, sums1, out)
    return out.reshape(row_tiles * TW, per_owner * TW), gradient


def solution(mesh):
    both = ("arc", "tile")
    in_specs = (
        P(both, None, None),
        P(both, None),
        P(both, None),
        P(both, None),
        P(both, None),
        P(),
        P("tile"),
        P("arc", "tile"),
    )
    return jax.shard_map(
        on_device,
        mesh=mesh,
        in_specs=in_specs,
        out_specs=(P("arc", "tile"), P("tile")),
        check_vma=False,
    )
```

```python
import functools

import jax
import jax.numpy as jnp
from jax import lax
from jax.experimental import pallas as pl
from jax.experimental.pallas import tpu as pltpu
from jax.sharding import PartitionSpec as P


HUBER = 1.345
TW = 128
SLOTS = 2
HEAD = 16
PARTS = (64, 64)
UNROLL = 8
BATCH = 6
ENTRY = 8
F32 = jnp.float32
BF16 = jnp.bfloat16
NT = (((1,), (1,)), ((), ()))


def prepare_kernel(owner_ref, design_ref, dt_ref, table_ref):
    blocks = design_ref.shape[0]

    @pl.loop(0, table_ref.shape[0])
    def _(i):
        table_ref[i] = -1

    @pl.loop(0, blocks * 4)
    def _(i):
        first = owner_ref[i] * SLOTS
        table_ref[jnp.where(table_ref[first] < 0, first, first + 1)] = i

    for b in range(blocks):
        for l in range(4):
            dt_ref[b * 4 + l] = design_ref[b, :, l * TW : (l + 1) * TW].T


def prepare(owner, design, n_owner):
    blocks = design.shape[0]
    vmem = pl.BlockSpec(memory_space=pltpu.VMEM)
    smem = pl.BlockSpec(memory_space=pltpu.SMEM)
    return pl.pallas_call(
        prepare_kernel,
        in_specs=[smem, vmem],
        out_specs=[vmem, smem],
        out_shape=[
            jax.ShapeDtypeStruct((blocks * 4, TW, TW), BF16),
            jax.ShapeDtypeStruct((n_owner * SLOTS,), jnp.int32),
        ],
        name="prepare",
    )(owner, design)


def weigh(
    owner_ref, sub_ref, sigma_ref, dt_ref, observed_ref, type_ref, all_ref, wt_ref, head_ref
):
    blocks = observed_ref.shape[0]
    head_ref[...] = jnp.zeros_like(head_ref)
    spread = jnp.zeros(observed_ref.shape, F32)
    for k in range(sigma_ref.shape[0]):
        spread = jnp.where(type_ref[...] == k, sigma_ref[k], spread)
    row = lax.broadcasted_iota(jnp.int32, (8, TW), 0)
    line = lax.broadcasted_iota(jnp.int32, (blocks, TW), 0)
    predicted = jnp.zeros((blocks, TW), F32)
    for b in range(blocks):
        parts = []
        for l in range(4):
            s = all_ref[owner_ref[b * 4 + l], pl.ds(sub_ref[b * 4 + l], 1), :]
            s = jnp.broadcast_to(s, (8, TW))
            hi = s.astype(BF16).astype(F32)
            mid = (s - hi).astype(BF16).astype(F32)
            low = s - hi - mid
            terms = jnp.where(row == 0, hi, jnp.where(row == 1, mid, low))
            terms = jnp.where(row < 3, terms, 0.0).astype(BF16)
            parts.append(jnp.dot(terms, dt_ref[b * 4 + l], preferred_element_type=F32))
        total = (parts[0] + parts[1]) + (parts[2] + parts[3])
        total = jnp.sum(total, axis=0, keepdims=True)
        predicted = jnp.where(line == b, total, predicted)
    residual = observed_ref[...] - predicted
    scaled = jnp.abs(residual) / spread
    root = jnp.sqrt(HUBER / jnp.maximum(scaled, HUBER)) / spread
    target = root * residual
    for b in range(blocks):
        head_ref[b, 0:1, :] = target[b : b + 1].astype(BF16)
        for l in range(4):
            tile = dt_ref[b * 4 + l].astype(F32)
            wt_ref[b * 4 + l] = (root[b : b + 1] * tile).astype(BF16)


def pack_kernel(chunk, table_ref, *refs):
    if chunk == 0:
        wt_ref, head_ref, out_ref = refs[-3:]

        @pl.when(pl.program_id(0) == 0)
        def _():
            weigh(*refs[:-1])

    else:
        wt_ref, head_ref, out_ref = refs
    step = pl.program_id(0)
    group = out_ref.shape[0]
    begin, part = sum(PARTS[:chunk]), PARTS[chunk]

    for g in range(group):
        item = table_ref[step * group + g]

        @pl.when(item >= 0)
        def _():
            b = item // 4
            m = item - b * 4
            base = 0
            if chunk == 0:
                out_ref[g, 0:TW, :] = wt_ref[item]
                base = TW
            if chunk == len(PARTS) - 1:
                out_ref[g, base : base + HEAD, :] = head_ref[b]
                base += HEAD
            for r in range(3):
                other = b * 4 + lax.rem(m + r + 1, 4)
                out_ref[g, base : base + part, :] = wt_ref[other, begin : begin + part, :]
                base += part


def payload_rows(chunk):
    rows = 3 * PARTS[chunk]
    return rows + TW * (chunk == 0) + HEAD * (chunk == len(PARTS) - 1)


def pack(chunk, table, *args):
    n_slot = table.shape[0]
    group = 16
    rows = payload_rows(chunk)
    whole = lambda x: pl.BlockSpec(x.shape, lambda i, *_: (0,) * len(x.shape))
    out_specs = [pl.BlockSpec((group, rows, TW), lambda i, *_: (i, 0, 0))]
    out_shape = [jax.ShapeDtypeStruct((n_slot, rows, TW), BF16)]
    if chunk == 0:
        dt, observed = args[3], args[4]
        kept = [
            jax.ShapeDtypeStruct(dt.shape, BF16),
            jax.ShapeDtypeStruct((observed.shape[0], HEAD, TW), BF16),
        ]
        smem = pl.BlockSpec(memory_space=pltpu.SMEM)
        in_specs = [smem] * 3 + [whole(x) for x in args[3:]]
        out_specs = [whole(x) for x in kept] + out_specs
        out_shape = kept + out_shape
    else:
        in_specs = [whole(x) for x in args]
    return pl.pallas_call(
        functools.partial(pack_kernel, chunk),
        grid_spec=pltpu.PrefetchScalarGridSpec(
            num_scalar_prefetch=1,
            grid=(n_slot // group,),
            in_specs=in_specs,
            out_specs=out_specs,
        ),
        out_shape=out_shape,
    )(table, *args)


def route_kernel(per_owner, n_arc, row_tiles, items, where_ref, all_ref, out_ref):
    ids = all_ref[:, per_owner, :].astype(jnp.int32)
    lane = lax.broadcasted_iota(jnp.int32, ids.shape, 1)
    own, arc = where_ref[0], where_ref[1]
    first = own * per_owner
    sub = ids - first
    hit = (sub >= 0) & (sub < per_owner) & (lane < items)
    taken = hit.astype(F32)
    k = lax.broadcasted_iota(jnp.int32, (TW, TW), 0)
    upper = (k < lax.broadcasted_iota(jnp.int32, (TW, TW), 1)).astype(F32)
    rank = jnp.dot(taken, upper, preferred_element_type=F32)
    half = row_tiles // 2
    columns = [sub]
    for r in range(4):
        ahead = pltpu.roll(ids, TW - r, 1) if r else ids
        behind = pltpu.roll(ids, 4 - r, 1) if r else ids
        tile = jnp.where(lane % 4 + r < 4, ahead, behind)
        high = jnp.zeros_like(tile)
        for a in range(1, n_arc):
            high += (tile >= a * row_tiles).astype(jnp.int32)
        row = tile - high * row_tiles
        side = (row >= half).astype(jnp.int32)
        distance = high - arc
        distance = jnp.where(distance < 0, distance + n_arc, distance)
        columns.append(((distance * 2 + side) * per_owner + sub) * half + row - side * half)
    dead = [per_owner] + [n_arc * row_tiles * per_owner] * 4
    out = jnp.zeros(out_ref.shape, F32)
    at = lax.broadcasted_iota(jnp.int32, out_ref.shape, 1)
    for slot in range(SLOTS):
        pick = jnp.where(rank == slot, taken, 0.0)
        live = jnp.sum(pick, axis=1, keepdims=True)
        for c, column in enumerate(columns):
            value = jnp.sum(pick * column.astype(F32), axis=1, keepdims=True)
            value += (1.0 - live) * dead[c]
            out = jnp.where(at == slot * ENTRY + c, value, out)
    out_ref[...] = out.astype(jnp.int32)


def route(where, everyone, per_owner, n_arc, row_tiles, items):
    n_owner = everyone.shape[0]
    vmem = pl.BlockSpec(memory_space=pltpu.VMEM)
    return pl.pallas_call(
        functools.partial(route_kernel, per_owner, n_arc, row_tiles, items),
        in_specs=[pl.BlockSpec(memory_space=pltpu.SMEM), vmem],
        out_specs=vmem,
        out_shape=jax.ShapeDtypeStruct((n_owner, SLOTS * ENTRY), jnp.int32),
        name="route",
    )(where, everyone)


def gather_kernel(chunk, table_ref, *refs):
    last = chunk == len(PARTS) - 1
    main_ref = refs[0]
    side_ref = refs[0] if chunk == 0 else refs[1]
    panels, firsts = refs[1 if chunk == 0 else 2 :][:2], refs[1 if chunk == 0 else 2 :][2:6]
    grad_ref = refs[-4] if last else None
    acc_ref, cast_ref, sems = refs[-3:]
    group = main_ref.shape[0]
    begin, part = sum(PARTS[:chunk]), PARTS[chunk]
    skip = HEAD if last else 0
    top = TW if chunk == 0 else 0
    step = pl.program_id(0)

    @pl.when(step == 0)
    def _():
        if last:
            grad_ref[...] = jnp.zeros_like(grad_ref)

        @pl.loop(0, cast_ref.shape[0] // BATCH)
        def _(i):
            for k in range(BATCH):
                acc_ref[i * BATCH + k] = jnp.zeros(acc_ref.shape[1:], F32)

    @pl.loop(0, group // UNROLL)
    def _(batch):
        prods = []
        for u in range(UNROLL):
            g = batch * UNROLL + u
            own = main_ref[g, 0:TW, :]
            at = g if chunk == 0 else step * group + g
            side = side_ref[at, top : top + skip + 3 * part, :]
            diag = main_ref[g, begin : begin + part, :]
            prods.append(
                [
                    lax.dot_general(x, own, NT, preferred_element_type=F32)
                    for x in (side, diag)
                ]
            )
        for u, (side, diag) in enumerate(prods):
            item = (step * group + batch * UNROLL + u) * ENTRY
            acc_ref[table_ref[item + 1]] += diag
            for r in range(3):
                acc_ref[table_ref[item + 2 + r]] += side[
                    skip + r * part : skip + (r + 1) * part
                ]
            if last:
                grad_ref[pl.ds(table_ref[item], 1), :] += side[0:1]

    @pl.when(step == pl.num_programs(0) - 1)
    def _():
        n_arc = sems.shape[0] // 2
        far = n_arc // 2
        piece = cast_ref.shape[0] // n_arc
        half = piece // 2
        alone = {(far, 0): 0, (far, 1): 1, (far + 1, 0): 2, (far - 1, 1): 3}
        near = [far, far + 1, far - 1]
        copies = []
        for p in near + [p for p in range(n_arc) if p not in near]:

            @pl.loop(0, piece // BATCH)
            def _(i):
                for k in range(BATCH):
                    at = p * piece + i * BATCH + k
                    cast_ref[at] = acc_ref[at].astype(BF16)

            for h in range(2):
                rows = pl.ds(p * piece + h * half, half)
                target = panels[h].at[pl.ds(p * half, half)]
                if (p, h) in alone:
                    target = firsts[alone[p, h]]
                copies.append(
                    pltpu.make_async_copy(cast_ref.at[rows], target, sems.at[2 * p + h])
                )
                copies[-1].start()
        for copy in copies:
            copy.wait()


def gather(chunk, table, got, n_tile_slots, n_arc):
    part = PARTS[chunk]
    group = 16
    n_slot = got[0].shape[0]
    main_rows = got[0].shape[1] if chunk == 0 else TW
    in_specs = [pl.BlockSpec((group, main_rows, TW), lambda i, *_: (i, 0, 0))]
    args = [got[0]]
    out_specs = [pl.BlockSpec(memory_space=pltpu.HBM)] * 6
    half = n_tile_slots // n_arc // 2
    out_shape = [
        jax.ShapeDtypeStruct((n, part, TW), BF16) for n in [half * n_arc] * 2 + [half] * 4
    ]
    if chunk > 0:
        in_specs.append(pl.BlockSpec(memory_space=pltpu.VMEM))
        args.append(pltpu.with_memory_space_constraint(got[chunk], pltpu.VMEM))
    if chunk == len(PARTS) - 1:
        out_specs.append(pl.BlockSpec((8, TW), lambda i, *_: (0, 0)))
        out_shape.append(jax.ShapeDtypeStruct((8, TW), F32))
    return pl.pallas_call(
        functools.partial(gather_kernel, chunk),
        grid_spec=pltpu.PrefetchScalarGridSpec(
            num_scalar_prefetch=1,
            grid=(n_slot // group,),
            in_specs=in_specs,
            out_specs=out_specs,
            scratch_shapes=[
                pltpu.VMEM((n_tile_slots + 1, part, TW), F32),
                pltpu.VMEM((n_tile_slots, part, TW), BF16),
                pltpu.SemaphoreType.DMA((2 * n_arc,)),
            ],
        ),
        out_shape=out_shape,
        compiler_params=pltpu.CompilerParams(
            vmem_limit_bytes=32 << 20
        ),
    )(table, *args)


def final_kernel(prior_ref, *refs):
    out_ref = refs[-1]
    n_row, step, width = prior_ref.shape
    per = width // TW
    half = n_row // 2
    at = pl.ds(pl.multiple_of(pl.program_id(0) * step, step), step)
    for h in range(2):
        own_ref, up_ref, down_ref = refs[3 * h : 3 * h + 3]
        for s in range(per):
            rows = slice(h * half, (h + 1) * half)
            cols = slice(s * TW, (s + 1) * TW)
            tiles = slice(s * half, (s + 1) * half)
            out_ref[rows, :, cols] = (
                prior_ref[rows, :, cols]
                + own_ref[tiles].astype(F32)
                + up_ref[tiles, at, :].astype(F32)
                + down_ref[tiles, at, :].astype(F32)
            )


def final(chunk, prior, sums, out):
    begin, part = sum(PARTS[:chunk]), PARTS[chunk]
    step = 16
    n_row, _, width = prior.shape
    per = sums[1].shape[0]
    spec = pl.BlockSpec((n_row, step, width), lambda i: (0, begin // step + i, 0))
    tiles = pl.BlockSpec((per, step, TW), lambda i: (0, i, 0))
    kept = pl.BlockSpec(memory_space=pltpu.VMEM)
    if out is not None:
        sums = [
            x if i % 3 == 0 else pltpu.with_memory_space_constraint(x, pltpu.VMEM)
            for i, x in enumerate(sums)
        ]
    args, alias = [prior, *sums], {}
    in_specs = [spec] + [tiles, kept, kept] * 2
    if out is not None:
        args.append(out)
        in_specs.append(pl.BlockSpec(memory_space=pl.ANY))
        alias = {len(args) - 1: 0}
    return pl.pallas_call(
        final_kernel,
        grid=(part // step,),
        in_specs=in_specs,
        out_specs=spec,
        out_shape=jax.ShapeDtypeStruct(prior.shape, F32),
        input_output_aliases=alias,
    )(*args)


def ring(panels, firsts, grad, n_arc):
    half = panels[0].shape[0] // n_arc
    far = n_arc // 2
    rising = [(i, (i + 1) % n_arc) for i in range(n_arc)]
    falling = [((i + 1) % n_arc, i) for i in range(n_arc)]
    add = lambda x, y: (x.astype(F32) + y.astype(F32)).astype(BF16)
    state = [[firsts[0], None], [None, firsts[1]]]
    for s in range(far):
        for h in range(2):
            up, down = state[h]
            own = lambda p: panels[h][p * half : (p + 1) * half]
            if s > h:
                up = add(own(far - s), up)
            elif s == 1:
                up = firsts[3]
            if s > 1 - h:
                down = add(own(far + s), down)
            elif s == 1:
                down = firsts[2]
            up, down = lax.optimization_barrier((up, down))
            if up is not None:
                up = lax.ppermute(up, "arc", rising)
            if down is not None:
                down = lax.ppermute(down, "arc", falling)
            up, down = lax.optimization_barrier((up, down))
            state[h] = [up, down]
        if grad is not None and 1 << s < n_arc:
            swap = [(i, i ^ (far >> s)) for i in range(n_arc)]
            grad = grad + lax.ppermute(grad, "arc", swap)
    return [panels[0], *state[0], panels[1], *state[1]], grad


def on_device(design, observed, obs_type, owner_of, sub_of, sigma_table, solution, prior):
    n_owner = lax.axis_size("tile")
    n_arc = lax.axis_size("arc")
    blocks = design.shape[0]
    per_owner = solution.shape[0] // TW
    tile_count = per_owner * n_owner
    row_tiles = tile_count // n_arc
    own_index = lax.axis_index("tile")
    arc_index = lax.axis_index("arc")

    tile_ids = (owner_of * per_owner + sub_of).reshape(blocks * 4)
    small = jnp.concatenate([solution, tile_ids.astype(F32)])
    small = jnp.pad(small, (0, 4 * TW - small.shape[0])).reshape(1, 4, TW)
    small = jnp.broadcast_to(small, (n_owner, 4, TW))
    everyone = lax.all_to_all(small, "tile", split_axis=0, concat_axis=0, tiled=True)

    owner, sub = owner_of.reshape(-1), sub_of.reshape(-1)
    dt, slots = prepare(owner, design, n_owner)
    wt, head, payload = pack(
        0, slots, owner, sub, sigma_table, dt, observed, obs_type, everyone
    )

    def send(p):
        p = p.reshape(n_owner, SLOTS, *p.shape[1:])
        g = lax.all_to_all(p, "tile", split_axis=0, concat_axis=0, tiled=True)
        return g.reshape(n_owner * SLOTS, *p.shape[2:])

    spare = tile_count * per_owner
    where = jnp.stack([own_index, arc_index]).astype(jnp.int32)
    table = route(where, everyone, per_owner, n_arc, row_tiles, blocks * 4).reshape(-1)

    got = []
    first = send(payload)
    (payload,) = pack(1, slots, wt, head)
    first, payload, table = lax.optimization_barrier((first, payload, table))
    got.append(first)
    outs = gather(0, table, got, spare, n_arc)
    got.append(send(payload))
    sums0, _ = ring(outs[:2], outs[2:6], None, n_arc)
    *outs, grad = gather(1, table, got, spare, n_arc)
    sums1, grad = ring(outs[:2], outs[2:6], grad, n_arc)
    gradient = grad[:per_owner].reshape(-1)

    prior = prior.reshape(row_tiles, TW, per_owner * TW)
    out = final(0, prior, sums0, None)
    out = final(1, prior, sums1, out)
    return out.reshape(row_tiles * TW, per_owner * TW), gradient


def solution(mesh):
    both = ("arc", "tile")
    in_specs = (
        P(both, None, None),
        P(both, None),
        P(both, None),
        P(both, None),
        P(both, None),
        P(),
        P("tile"),
        P("arc", "tile"),
    )
    return jax.shard_map(
        on_device,
        mesh=mesh,
        in_specs=in_specs,
        out_specs=(P("arc", "tile"), P("tile")),
        check_vma=False,
    )
```
